512 devices in a mesh: seq: 64 (over y, z), exp: 8 (over x, core).
Axes of the slice: x: 4, y: 4, z: 16, core: 2. Of those that a mesh axis runs over, the one named last changes fastest.
Arguments:
- tokens: bfloat16 [4096, 128], P('seq'), may hold values from -36 to 36
- norm_gains: float32 [2, 4096], P(None, 'seq'), may hold values from 0.1 to 1.9
- q_weight: bfloat16 [4096, 4096], P('seq', 'exp'), may hold values from -16 to 16
- kv_weight: bfloat16 [4096, 2, 1024], P('seq', None, 'exp'), may hold values from -1 to 1
- out_weight: bfloat16 [4096, 4096], P('seq', 'exp'), may hold values from -0.3 to 0.3
- kv_cache: bfloat16 [2, 512, 256, 1024], P(None, 'seq', None, 'exp'), may hold values from -8 to 8
- block_count: int32 [32], replicated, may hold values from 1 to 128, 512 in all
- placement: int32 [512], P('seq'), may hold values from 0 to 511, each once
- block_live: int32 [512], P('seq'), may hold values 0 or 1
- router_weight: bfloat16 [4096, 8], P('seq'), may hold values from -0.09375 to 0.09375
- routes: int32 [128, 2], replicated, may hold values from 0 to 7, all different within a row
- expert_in: bfloat16 [8, 2, 4096, 7168], P(None, None, 'seq', 'exp'), may hold values from -0.09375 to 0.09375
- expert_out: bfloat16 [8, 4096, 7168], P(None, 'seq', 'exp'), may hold values from -0.0625 to 0.0625
Outputs:
- layer_out: bfloat16 [4096, 128], P('seq')
The draws below stay inside these ranges and needn't reach their ends.
Inputs may be any that keep to these rules, and one draw needn't show every extreme that they name: `block_count`: the counts sum to 512; the longest request holds exactly 128 blocks. `placement`: each pool slot holds a different block. `routes`: each row names two different experts.
All inputs are finite; a program needn't handle non-finite values. No bound on the sum of `block_live` on one device may be relied on, other than what follows from the above.
Results may differ from the reference program's by a relative error of at most 0.0065.
Values may be sent and summed in bfloat16 or wider, within the bound.
A program may use at most 128 MiB of HBM per device.

```python
import math
import jax
import jax.numpy as jnp
import numpy as np
from jax import lax

D = 4096
HEADS = 32
KV_HEADS = 8
HEAD_DIM = 128
EXPERTS = 8
FF = 7168
TOPK = 2
STEPS = 4
BLOCK = 256
REQS = 32
ROWS = 128
NBLK = 512
MOST_BLK = 128


def value_signs(key):
    return jax.random.rademacher(jax.random.fold_in(key, 53), (KV_HEADS * HEAD_DIM,), jnp.float32)


def draw_tokens(key, part):
    column = jnp.arange(D, dtype=jnp.float32) / max(D - 1, 1)
    row_key = jax.random.fold_in(key, 3)
    base_values = jax.random.truncated_normal(key, -4.0, 4.0, (D, ROWS), jnp.float32)
    row_scale = jnp.exp(jax.random.uniform(row_key, (1, ROWS), jnp.float32, -0.35, 0.35))
    column_scale = 3.0 ** (column - 0.5)
    drawn = base_values * column_scale[:, None] * row_scale
    return drawn.astype(jnp.bfloat16)


def shared_keys(key):
    return jax.random.truncated_normal(jax.random.fold_in(key, 11), -4.0, 4.0, (D, KV_HEADS, HEAD_DIM), jnp.float32)


def draw_kv_weight(key, part):
    key_part = shared_keys(key) / math.sqrt(D)
    key_part = key_part.reshape(D, KV_HEADS * HEAD_DIM)
    value_part = jax.random.truncated_normal(jax.random.fold_in(key, 12), -4.0, 4.0, (D, KV_HEADS * HEAD_DIM), jnp.float32) / math.sqrt(D)
    stacked = jnp.stack([key_part, value_part], axis=1)
    return stacked.astype(jnp.bfloat16)


def draw_q_weight(key, part):
    group_size = HEADS // KV_HEADS
    random_part = jax.random.truncated_normal(jax.random.fold_in(key, 13), -4.0, 4.0, (D, HEADS, HEAD_DIM), jnp.float32)
    aligned = jnp.repeat(shared_keys(key), group_size, axis=1)
    strength = jax.random.uniform(jax.random.fold_in(key, 14), (HEADS,), jnp.float32, 0.3, 0.8)
    drawn = (strength[None, :, None] * aligned + random_part).reshape(D, HEADS * HEAD_DIM) / math.sqrt(D)
    return drawn.astype(jnp.bfloat16)


def draw_out_weight(key, part):
    width = HEADS * HEAD_DIM
    group_size = HEADS // KV_HEADS
    random_part = jax.random.truncated_normal(jax.random.fold_in(key, 41), -4.0, 4.0, (D, width), jnp.float32) / math.sqrt(width)
    column_signs = jnp.repeat(value_signs(key).reshape(KV_HEADS, HEAD_DIM), group_size, axis=0).reshape(width)
    feature_signs = jax.random.rademacher(jax.random.fold_in(key, 42), (D,), jnp.float32)
    drawn = random_part + 2.4 / width * feature_signs[:, None] * column_signs[None, :]
    return drawn.astype(jnp.bfloat16)


def draw_kv_cache(key, part):
    width = KV_HEADS * HEAD_DIM
    key_rows = jax.random.truncated_normal(jax.random.fold_in(key, 31), -6.0, 6.0, (NBLK, BLOCK, width), jnp.float32)
    value_rows = jax.random.truncated_normal(jax.random.fold_in(key, 32), -6.0, 6.0, (NBLK, BLOCK, width), jnp.float32)
    value_rows = value_rows + 0.5 * value_signs(key)[None, None, :]
    return jnp.stack([key_rows, value_rows], axis=0).astype(jnp.bfloat16)


def with_ends(entries, rng, low, top_value):
    longest = entries.shape.index(max(entries.shape))
    spots = []
    for shift in (0, 1):
        where = [jax.random.randint(jax.random.fold_in(rng, axis), (), 0, length) for axis, length in enumerate(entries.shape)]
        where[longest] = (where[longest] + shift) % entries.shape[longest]
        spots.append(tuple(where))
    return entries.at[spots[0]].set(low).at[spots[1]].set(top_value)


def shard_levels(own_key, shape, split, smallest, high):
    def one(position, parts):
        steps = jax.random.uniform(jax.random.fold_in(jax.random.fold_in(own_key, 6), position), (parts,), jnp.float32, smallest / len(split), high / len(split))
        return jnp.repeat(jnp.exp(steps), shape[position] // parts).reshape((-1,) + (1,) * (len(shape) - position - 1))

    loudness = one(*split[0])
    for cut in split[1:]:
        loudness = loudness * one(*cut)
    return loudness


def different_ones(rng, rows, number_of, top, lift):
    ranking = jax.random.permutation(jax.random.fold_in(rng, 1), number_of)
    pull = ranking
    for power in range(3):
        pull = pull * pull // number_of
    pull = pull * lift // number_of
    tickets = jax.random.randint(jax.random.fold_in(rng, 2), (rows, number_of), 0, 4096) + pull
    holders = jax.random.permutation(jax.random.fold_in(rng, 3), rows)[jnp.arange(number_of) % rows]
    tickets = jnp.where(jnp.arange(rows)[:, None] == holders[None, :], 1 << 14, tickets)
    priority = tickets * number_of + jnp.arange(number_of)
    return lax.top_k(priority.astype(jnp.int32), top)[1].astype(jnp.int32)


def split_up(count, total, limit, lean):
    loads = [(1 << 20) // math.isqrt(standing ** lean) + 1 for standing in range(2, count + 1)]
    rest, holding = total - limit - (count - 1), [1] * (count - 1)
    while rest > 0:
        movable = [i for i in range(count - 1) if holding[i] < limit]
        whole, remaining = sum([loads[i] for i in movable]), rest
        for i in movable:
            more = min(limit - holding[i], max(1, remaining * loads[i] // whole), rest)
            holding[i] = holding[i] + more
            rest = rest - more
    return np.array([limit] + holding)


def uneven_parts(rng, count, total, reach, lean):
    if count == 2:
        one = jax.random.randint(rng, (), max(1, total - reach), min(reach, total - 1) + 1)
        return jnp.stack([one, total - one])
    lengths = jnp.asarray(split_up(count, total, reach, lean), jnp.int32)
    pairs = (count - 1) // 2
    giver, receiver = lengths[1:1 + 2 * pairs:2], lengths[2:2 + 2 * pairs:2]
    room = jnp.minimum(giver - 1, reach - receiver)
    shifted = jax.random.randint(jax.random.fold_in(rng, 1), (pairs,), 0, 1 << 20) % (room + 1)
    lengths = lengths.at[1:1 + 2 * pairs:2].set(giver - shifted).at[2:2 + 2 * pairs:2].set(receiver + shifted)
    return lengths[jax.random.permutation(jax.random.fold_in(rng, 2), count)]


def bell_draw(key, shape, scale, most, shards=(), held_as=jnp.bfloat16):
    entries = scale * jax.random.normal(key, shape, jnp.float32)
    if shards:
        entries = entries * shard_levels(key, shape, shards, -0.22, 0.18)
    return jnp.clip(entries, -most, most).astype(held_as)


def setup_inputs(seed: int = 0) -> dict:
    seeds = jax.random.split(jax.random.key(seed), 14)
    tokens = draw_tokens(jax.random.fold_in(seeds[13], 71), 0)
    norm_gains = jnp.clip(1.0 + 0.18 * jax.random.normal(seeds[1], (2, D), jnp.float32), 0.1, 1.9)
    q_weight = draw_q_weight(jax.random.fold_in(seeds[13], 71), 0)
    kv_weight = draw_kv_weight(jax.random.fold_in(seeds[13], 71), 0)
    out_weight = draw_out_weight(jax.random.fold_in(seeds[13], 71), 0)
    kv_cache = draw_kv_cache(jax.random.fold_in(seeds[13], 71), 0)
    block_count = uneven_parts(seeds[6], REQS, NBLK, MOST_BLK, 2).astype(jnp.int32)
    placement = jax.random.permutation(seeds[7], NBLK).astype(jnp.int32)
    block_live = with_ends((jax.random.randint(seeds[8], (NBLK,), 0, 4) < 3).astype(jnp.int32), jax.random.fold_in(seeds[8], 1), 0, 1)
    router_weight = bell_draw(seeds[9], (D, EXPERTS), D ** -0.5, 0.09375, ((0, 64),))
    routes = different_ones(seeds[10], ROWS, EXPERTS, TOPK, 4096)
    expert_in = bell_draw(seeds[11], (EXPERTS, 2, D, FF), D ** -0.5, 0.09375, ((2, 64), (3, 8)))
    expert_out = bell_draw(seeds[12], (EXPERTS, D, FF), FF ** -0.5, 0.0625, ((1, 64), (2, 8)))
    return dict(tokens=tokens, norm_gains=norm_gains, q_weight=q_weight, kv_weight=kv_weight, out_weight=out_weight, kv_cache=kv_cache, block_count=block_count, placement=placement, block_live=block_live, router_weight=router_weight, routes=routes, expert_in=expert_in, expert_out=expert_out)


NEGATIVE = -1e+30
EPSILON = 1e-05

def rounded(value):
    return lax.optimization_barrier(value.astype(jnp.bfloat16)).astype(jnp.float32)

def block_owners(block_count, placement):
    starts = jnp.cumsum(block_count) - block_count
    before = (starts[None, :] <= placement[:, None]).astype(jnp.int32)
    return lax.optimization_barrier(jnp.sum(before, axis=1)) - 1

def softmax_join(first_part, second_part):
    joined_top = jnp.maximum(first_part[0], second_part[0])
    first_factor = jnp.exp(first_part[0] - joined_top)
    second_factor = jnp.exp(second_part[0] - joined_top)
    joined_total = first_part[1] * first_factor + second_part[1] * second_factor
    joined_sum = first_part[2] * first_factor[..., None] + second_part[2] * second_factor[..., None]
    return (joined_top, joined_total, joined_sum)

def reference(tokens, norm_gains, q_weight, kv_weight, out_weight, kv_cache, block_count, placement, block_live, router_weight, routes, expert_in, expert_out):
    highest = lax.Precision.HIGHEST
    group_size = HEADS // KV_HEADS
    score_scale = 1.0 / math.sqrt(HEAD_DIM)
    token_float = tokens.astype(jnp.float32)
    attn_rms = lax.rsqrt(lax.optimization_barrier(jnp.sum(token_float * token_float, axis=0)) / D + EPSILON)
    normed = (token_float * norm_gains[0][:, None]).astype(jnp.bfloat16)
    queries = rounded(jnp.dot(normed.T, q_weight, preferred_element_type=jnp.float32) * attn_rms[:, None])
    fresh_rows = rounded(jnp.dot(normed.T, kv_weight.reshape(D, 2 * KV_HEADS * HEAD_DIM), preferred_element_type=jnp.float32) * attn_rms[:, None])
    queries = queries.reshape(STEPS, REQS, KV_HEADS, group_size, HEAD_DIM)
    fresh_rows = fresh_rows.reshape(STEPS, REQS, 2, KV_HEADS, HEAD_DIM)
    new_keys = fresh_rows[:, :, 0]
    new_values = fresh_rows[:, :, 1]
    cache_keys = kv_cache[0].astype(jnp.float32).reshape(NBLK, BLOCK, KV_HEADS, HEAD_DIM)
    cache_values = kv_cache[1].astype(jnp.float32).reshape(NBLK, BLOCK, KV_HEADS, HEAD_DIM)
    block_owner = block_owners(block_count, placement)
    picked = queries[:, block_owner]
    block_scores = jnp.einsum('tpkgd,pjkd->pkgtj', picked, cache_keys, precision=highest) * score_scale
    block_top = lax.optimization_barrier(jnp.max(block_scores, axis=-1))
    block_weights = rounded(jnp.exp(block_scores - block_top[..., None]))
    block_total = lax.optimization_barrier(jnp.sum(block_weights, axis=-1))
    block_sum = jnp.einsum('pkgtj,pjkd->pkgtd', block_weights, cache_values, precision=highest)
    block_alive = (block_live == 1)[:, None, None, None]
    block_top = jnp.where(block_alive, block_top, NEGATIVE)
    block_total = jnp.where(block_alive, block_total, 0.0)
    block_sum = jnp.where(block_alive[..., None], block_sum, 0.0)
    member = (block_owner[:, None] == jnp.arange(REQS)[None, :])[:, :, None, None, None]
    request_top = lax.optimization_barrier(jnp.max(jnp.where(member, block_top[:, None], NEGATIVE), axis=0))
    factor = jnp.where(member, jnp.exp(jnp.where(member, block_top[:, None] - request_top[None], NEGATIVE)), 0.0)
    request_total = lax.optimization_barrier(jnp.sum(factor * block_total[:, None], axis=0))
    request_sum = jnp.einsum('prkgt,pkgtd->rkgtd', factor, block_sum, precision=highest)
    new_scores = jnp.einsum('trkgd,srkd->rkgts', queries, new_keys, precision=highest) * score_scale
    causal = jnp.arange(STEPS)[:, None] >= jnp.arange(STEPS)[None, :]
    new_scores = jnp.where(causal, new_scores, NEGATIVE)
    new_top = lax.optimization_barrier(jnp.max(new_scores, axis=-1))
    new_weights = rounded(jnp.where(causal, jnp.exp(new_scores - new_top[..., None]), 0.0))
    new_total = lax.optimization_barrier(jnp.sum(new_weights, axis=-1))
    new_sum = jnp.einsum('rkgts,srkd->rkgtd', new_weights, new_values, precision=highest)
    joined_top, joined_total, joined_sum = softmax_join((request_top, request_total, request_sum), (new_top, new_total, new_sum))
    attention = (joined_sum / joined_total[..., None]).astype(jnp.bfloat16)
    attention = jnp.transpose(attention, (3, 0, 1, 2, 4)).reshape(ROWS, HEADS * HEAD_DIM)
    residual = token_float + jnp.dot(out_weight, attention.T, preferred_element_type=jnp.float32)
    moe_rms = lax.rsqrt(lax.optimization_barrier(jnp.sum(residual * residual, axis=0)) / D + EPSILON)
    hidden_in = (residual * norm_gains[1][:, None]).astype(jnp.bfloat16)
    all_logits = jnp.dot(hidden_in.T, router_weight, preferred_element_type=jnp.float32)
    logits = jnp.take_along_axis(all_logits, routes, axis=1) * moe_rms[:, None]
    sigmoids = jax.nn.sigmoid(logits)
    gate_weights = sigmoids / lax.optimization_barrier(jnp.sum(sigmoids, axis=1, keepdims=True))
    hidden_float = hidden_in.astype(jnp.float32)
    expert_inputs = jnp.zeros((ROWS, TOPK, 2, FF), jnp.float32)
    for expert in range(EXPERTS):
        product = jnp.einsum('di,cdf->icf', hidden_float, expert_in[expert].astype(jnp.float32), precision=highest)
        expert_inputs = jnp.where((routes == expert)[:, :, None, None], product[:, None], expert_inputs)
    expert_inputs = expert_inputs * moe_rms[:, None, None, None]
    activations = (jax.nn.silu(expert_inputs[:, :, 0]) * expert_inputs[:, :, 1]).astype(jnp.bfloat16)
    activations = activations.reshape(ROWS * TOPK, FF)
    flat_routes = routes.reshape(ROWS * TOPK)
    down_rows = jnp.zeros((D, ROWS * TOPK), jnp.float32)
    for expert in range(EXPERTS):
        product = jnp.dot(expert_out[expert], activations.T, preferred_element_type=jnp.float32)
        down_rows = jnp.where((flat_routes == expert)[None, :], product, down_rows)
    expert_total = lax.optimization_barrier(jnp.sum(down_rows.reshape(D, ROWS, TOPK) * gate_weights[None], axis=2))
    return (residual + expert_total).astype(jnp.bfloat16)
```

```python
import functools
import math

import jax
import jax.numpy as jnp
from jax import lax
from jax.experimental import pallas as pl
from jax.experimental.pallas import tpu as pltpu
from jax.sharding import PartitionSpec as P

HEAD_DIM = 128
TOPK = 2
LANES = 128
NEGATIVE = -1e30
EPSILON = 1e-05
MESH = pl.DeviceIdType.MESH
HIGHEST = lax.Precision.HIGHEST
FIRST = (((0,), (0,)), ((), ()))
LAST = (((1,), (1,)), ((), ()))
F32 = jnp.float32
BF16 = jnp.bfloat16


def dot(first, second, dims, precision=None):
    return lax.dot_general(
        first, second, dims, precision=precision, preferred_element_type=F32
    )


def ring_order(count):
    return sorted(range(1, count), key=lambda d: -min(d, count - d))


def kernel(
    cfg,
    same_ref,
    live_ref,
    tok_ref,
    gains_ref,
    qw_ref,
    kvw_ref,
    ow_ref,
    cache_ref,
    sel_ref,
    lead_ref,
    router_ref,
    routes_ref,
    onehot_ref,
    ein_ref,
    eout_ref,
    out_ref,
    a_sy,
    a_ry,
    a_sz,
    a_rz,
    a_g,
    e_sy,
    e_ry,
    e_sz,
    e_rz,
    e_g,
    b_sy,
    b_ry,
    b_sz,
    b_rz,
    b_g,
    x_s1,
    x_r1,
    x_s2,
    x_r2,
    y_send,
    z_send,
    x_send,
    y_recv,
    z_recv,
    x_recv,
):
    ny, nz, nx, depth, steps = cfg
    rows = tok_ref.shape[1]
    ry = rows // ny
    rp = ry // nz
    heads = qw_ref.shape[1] // HEAD_DIM
    qcols = heads * HEAD_DIM
    kcols = qcols + HEAD_DIM
    vcols = kcols + HEAD_DIM
    blocks = cache_ref.shape[1]
    experts = ein_ref.shape[0]
    ff = ein_ref.shape[3]
    scale = 1.0 / math.sqrt(HEAD_DIM)
    seq = lax.axis_index("seq")
    e = lax.axis_index("exp")
    y = lax.div(seq, nz)
    z = lax.rem(seq, nz)

    def y_peer(d):
        return lax.rem(y + d, ny)

    def z_peer(d):
        return lax.rem(z + d, nz)

    def x_peer(d):
        return lax.rem(e + d, nx)

    def y_copy(src, dst, d, phase):
        return pltpu.make_async_remote_copy(
            src_ref=src,
            dst_ref=dst,
            send_sem=y_send.at[d - 1],
            recv_sem=y_recv.at[phase, d - 1],
            device_id=(y_peer(d) * nz + z, e),
            device_id_type=MESH,
        )

    def z_copy(src, dst, d, phase):
        return pltpu.make_async_remote_copy(
            src_ref=src,
            dst_ref=dst,
            send_sem=z_send.at[d - 1],
            recv_sem=z_recv.at[phase, d - 1],
            device_id=(y * nz + z_peer(d), e),
            device_id_type=MESH,
        )

    def run(copies):
        for copy in copies:
            copy.start()
        for copy in copies:
            copy.wait()

    def y_exchange(send, recv, phase):
        recv[y] = send[y]
        run([y_copy(send.at[y_peer(d)], recv.at[y], d, phase) for d in ring_order(ny)])

    def z_exchange(send, recv, phase):
        recv[z] = send[z]
        run([z_copy(send.at[z_peer(d)], recv.at[z], d, phase) for d in ring_order(nz)])

    def gather(held, phase):
        run([z_copy(held.at[y, z], held.at[y, z], d, phase) for d in ring_order(nz)])
        run([y_copy(held.at[y], held.at[y], d, phase) for d in ring_order(ny)])

    def x_reduce(part, send, recv, phase):
        send[...] = part.astype(BF16)
        recv[e] = part.astype(BF16)
        run(
            [
                pltpu.make_async_remote_copy(
                    src_ref=send,
                    dst_ref=recv.at[e],
                    send_sem=x_send.at[d - 1],
                    recv_sem=x_recv.at[phase, d - 1],
                    device_id=(seq, x_peer(d)),
                    device_id_type=MESH,
                )
                for d in ring_order(nx)
            ]
        )
        total = recv[0].astype(F32)
        for index in range(1, nx):
            total = total + recv[index].astype(F32)
        return total

    barrier = pltpu.get_barrier_semaphore()
    for d in range(1, ny):
        pl.semaphore_signal(barrier, inc=1, device_id=(y_peer(d) * nz + z, e), device_id_type=MESH)
    for d in range(1, nz):
        pl.semaphore_signal(barrier, inc=1, device_id=(y * nz + z_peer(d), e), device_id_type=MESH)
    for d in range(1, nx):
        pl.semaphore_signal(barrier, inc=1, device_id=(seq, x_peer(d)), device_id_type=MESH)

    def lane_of(count):
        return lax.broadcasted_iota(jnp.int32, (count, LANES), 1)

    def by_head(columns):
        count = columns[0].shape[0]
        lane = lax.rem(lane_of(count), heads)
        spread = jnp.broadcast_to(columns[0], (count, LANES))
        for h in range(1, heads):
            spread = jnp.where(lane == h, columns[h], spread)
        return spread

    def pack_stats(top, total):
        group = lax.div(lane_of(top.shape[0]), heads)
        high = top.astype(BF16).astype(F32)
        rest = top - high
        middle = rest.astype(BF16).astype(F32)
        total_high = total.astype(BF16).astype(F32)
        packed = jnp.where(group == 0, high, total - total_high)
        packed = jnp.where(group == 1, middle, packed)
        packed = jnp.where(group == 2, rest - middle, packed)
        packed = jnp.where(group == 3, total_high, packed)
        return packed.astype(BF16)

    def stat(values, group, h):
        lane = qcols + group * heads + h
        return values[..., lane : lane + 1]

    def unpack(values, h):
        top = (stat(values, 0, h) + stat(values, 1, h)) + stat(values, 2, h)
        total = stat(values, 3, h) + stat(values, 4, h)
        return top, total, values[..., h * HEAD_DIM : (h + 1) * HEAD_DIM]

    tok = tok_ref[...].astype(F32)
    ones = jnp.ones((tok.shape[0], LANES), F32)
    normed = (tok * gains_ref[:, 0:1]).astype(BF16)
    q_part = dot(normed, qw_ref[...], FIRST)
    kv_part = dot(normed, kvw_ref[...], FIRST)
    squares = dot(tok * tok, ones, FIRST, HIGHEST)
    for part in range(ny):
        here = slice(part * ry, (part + 1) * ry)
        a_sy[part, :, 0:qcols] = q_part[here].astype(BF16)
        a_sy[part, :, qcols:vcols] = kv_part[here].astype(BF16)
        a_sy[part, :, vcols : vcols + LANES] = squares[here].astype(BF16)

    pl.semaphore_wait(barrier, (ny - 1) + (nz - 1) + (nx - 1))
    y_exchange(a_sy, a_ry, 0)
    part_sum = a_ry[0].astype(F32)
    for part in range(1, ny):
        part_sum = part_sum + a_ry[part].astype(F32)
    a_sz[...] = part_sum.reshape(nz, rp, part_sum.shape[1]).astype(BF16)
    z_exchange(a_sz, a_rz, 0)
    fresh = jnp.sum(a_rz[...].astype(F32), axis=0)
    attn_rms = lax.rsqrt(fresh[:, vcols : vcols + 1] / depth + EPSILON)
    own = (fresh[:, 0:vcols] * attn_rms).astype(BF16)
    a_g[y, z] = own
    gather(a_g, 1)
    fresh_rows = a_g[...].astype(F32).reshape(rows, vcols).astype(BF16)

    sel = sel_ref[...]
    picked = [
        dot(sel.astype(BF16), fresh_rows[:, h * HEAD_DIM : (h + 1) * HEAD_DIM], (((1,), (0,)), ((), ())))
        for h in range(heads)
    ]
    tops, totals, sums = [], [], []
    for p in range(blocks):
        here = slice(p * 8, (p + 1) * 8)
        block_query = jnp.concatenate([picked[h][here] for h in range(heads)], axis=0)
        scores = dot(block_query.astype(BF16), cache_ref[0, p], LAST) * scale
        top = jnp.max(scores, axis=1, keepdims=True)
        weights = jnp.exp(scores - top).astype(BF16)
        total = jnp.sum(weights.astype(F32), axis=1, keepdims=True)
        weighted = dot(weights, cache_ref[1, p], (((1,), (0,)), ((), ())))
        alive = live_ref[p]
        top = by_head([top[h * 8 : (h + 1) * 8] for h in range(heads)])
        tops.append(top * alive + (1.0 - alive) * NEGATIVE)
        totals.append(by_head([total[h * 8 : (h + 1) * 8] for h in range(heads)]) * alive)
        sums.append(weighted * alive)
    joint, factors = [], []
    for p in range(blocks):
        best = tops[p]
        for q in range(blocks):
            if q != p:
                best = jnp.maximum(best, tops[q] + same_ref[p * blocks + q])
        joint.append(best)
        factors.append(jnp.exp(tops[p] - best))
    local_total = dot(
        sel, jnp.concatenate([totals[p] * factors[p] for p in range(blocks)], axis=0), FIRST, HIGHEST
    )
    lead = lead_ref[...]
    local_top = dot(lead, jnp.concatenate(joint, axis=0), FIRST, HIGHEST)
    present = dot(lead, jnp.ones((lead.shape[0], LANES), F32), FIRST)
    local_top = jnp.where(present > 0.5, local_top, NEGATIVE)
    local_stats = pack_stats(local_top, local_total)
    local_sums = [
        dot(
            sel,
            jnp.concatenate(
                [sums[p][h * 8 : (h + 1) * 8] * factors[p][:, h : h + 1] for p in range(blocks)],
                axis=0,
            ),
            FIRST,
            HIGHEST,
        )
        for h in range(heads)
    ]
    for part in range(ny):
        here = slice(part * ry, (part + 1) * ry)
        for h in range(heads):
            e_sy[part, :, h * HEAD_DIM : (h + 1) * HEAD_DIM] = local_sums[h][here].astype(BF16)
        e_sy[part, :, qcols : qcols + LANES] = local_stats[here]
    y_exchange(e_sy, e_ry, 2)
    parts = [e_ry[part].astype(F32) for part in range(ny)]
    tops, totals = [], []
    for h in range(heads):
        pieces = [unpack(values, h) for values in parts]
        top = functools.reduce(jnp.maximum, [piece[0] for piece in pieces])
        total, weighted = 0.0, 0.0
        for piece in pieces:
            factor = jnp.exp(piece[0] - top)
            total = total + factor * piece[1]
            weighted = weighted + factor * piece[2]
        tops.append(top)
        totals.append(total)
        e_sz[:, :, h * HEAD_DIM : (h + 1) * HEAD_DIM] = weighted.reshape(nz, rp, HEAD_DIM).astype(BF16)
    stats = pack_stats(by_head(tops), by_head(totals)).astype(F32)
    e_sz[:, :, qcols : qcols + LANES] = stats.reshape(nz, rp, LANES).astype(BF16)
    z_exchange(e_sz, e_rz, 2)
    values = e_rz[...].astype(F32)
    own = own.astype(F32)
    new_rows = [a_g[s, z].astype(F32) for s in range(steps)]
    attended = []
    for h in range(heads):
        tops, totals, sums = unpack(values, h)
        top = jnp.max(tops, axis=0)
        factors = jnp.exp(tops - top[None])
        total = jnp.sum(factors * totals, axis=0)
        weighted = jnp.sum(factors * sums, axis=0)
        query = own[:, h * HEAD_DIM : (h + 1) * HEAD_DIM]
        scores = []
        for s in range(steps):
            score = jnp.sum(query * new_rows[s][:, qcols:kcols], axis=1, keepdims=True) * scale
            scores.append(jnp.where(y >= s, score, NEGATIVE))
        new_top = functools.reduce(jnp.maximum, scores)
        joined = jnp.maximum(top, new_top)
        new_total, new_sum = 0.0, 0.0
        for s in range(steps):
            weight = jnp.where(y >= s, jnp.exp(scores[s] - new_top), 0.0)
            weight = weight.astype(BF16).astype(F32)
            new_total = new_total + weight
            new_sum = new_sum + weight * new_rows[s][:, kcols:vcols]
        old_factor = jnp.exp(top - joined)
        new_factor = jnp.exp(new_top - joined)
        total = total * old_factor + new_total * new_factor
        weighted = weighted * old_factor + new_sum * new_factor
        attended.append(weighted / total)
    e_g[y, z] = jnp.concatenate(attended, axis=1).astype(BF16)
    gather(e_g, 3)
    attention = e_g[...].astype(F32).reshape(rows, qcols).astype(BF16)

    head_part = dot(ow_ref[...], attention, LAST)
    residual = tok + x_reduce(head_part, x_s1, x_r1, 0)

    hidden = (residual * gains_ref[:, 1:2]).astype(BF16)
    logits = dot(hidden, router_ref[...], FIRST)
    squares = dot(residual * residual, ones, FIRST, HIGHEST)
    stats = jnp.where(lane_of(rows) < experts, logits, squares).astype(BF16)
    hidden_float = hidden.astype(F32)
    masked = [
        jnp.concatenate(
            [
                jnp.where(routes_ref[k : k + 1, :] == expert, hidden_float, 0.0)
                for expert in range(experts)
            ],
            axis=0,
        )
        for k in range(TOPK)
    ]
    masked = jnp.concatenate(masked, axis=1).astype(BF16)
    for c in range(2):
        weight = ein_ref[:, c].reshape(experts * ein_ref.shape[2], ff)
        product = dot(masked, weight, FIRST)
        for part in range(ny):
            for k in range(TOPK):
                start = k * rows + part * ry
                b_sy[part, k * ry : (k + 1) * ry, c * ff : (c + 1) * ff] = product[
                    start : start + ry
                ].astype(BF16)
    for part in range(ny):
        for k in range(TOPK):
            b_sy[part, k * ry : (k + 1) * ry, 2 * ff : 2 * ff + LANES] = stats[
                part * ry : (part + 1) * ry
            ]
    y_exchange(b_sy, b_ry, 4)
    part_sum = b_ry[0].astype(F32)
    for part in range(1, ny):
        part_sum = part_sum + b_ry[part].astype(F32)
    for k in range(TOPK):
        b_sz[:, k] = part_sum[k * ry : (k + 1) * ry].reshape(nz, rp, part_sum.shape[1]).astype(BF16)
    z_exchange(b_sz, b_rz, 4)
    inputs = [jnp.sum(b_rz[:, k].astype(F32), axis=0) for k in range(TOPK)]
    moe_rms = lax.rsqrt(inputs[0][:, 2 * ff + 64 : 2 * ff + 65] / depth + EPSILON)
    sigmoids = []
    for k in range(TOPK):
        chosen = inputs[0][:, 2 * ff : 2 * ff + LANES] * onehot_ref[seq, k]
        logit = jnp.sum(chosen, axis=1, keepdims=True) * moe_rms
        sigmoids.append(1.0 / (1.0 + jnp.exp(-logit)))
    for k in range(TOPK):
        gate = inputs[k][:, 0:ff] * moe_rms
        up = inputs[k][:, ff : 2 * ff] * moe_rms
        active = gate / (1.0 + jnp.exp(-gate)) * up
        b_g[y, z, k] = (active * (sigmoids[k] / (sigmoids[0] + sigmoids[1]))).astype(BF16)
    gather(b_g, 5)
    expert_part = jnp.zeros(residual.shape, F32)
    for k in range(TOPK):
        active = b_g[:, :, k].astype(F32).reshape(rows, ff).astype(BF16)
        for expert in range(experts):
            product = dot(eout_ref[expert], active, LAST)
            expert_part = expert_part + jnp.where(routes_ref[k : k + 1, :] == expert, product, 0.0)
    out_ref[...] = (residual + x_reduce(expert_part, x_s2, x_r2, 1)).astype(BF16)


def block_owners(block_count, placement):
    starts = jnp.cumsum(block_count) - block_count
    before = (starts[None, :] <= placement[:, None]).astype(jnp.int32)
    return jnp.sum(before, axis=1) - 1


def per_device(
    nx,
    seq_size,
    tokens,
    norm_gains,
    q_weight,
    kv_weight,
    out_weight,
    kv_cache,
    block_count,
    placement,
    block_live,
    router_weight,
    routes,
    expert_in,
    expert_out,
):
    width, rows = tokens.shape
    requests = block_count.shape[0]
    steps = rows // requests
    ny, nz = steps, seq_size // steps
    rp = rows // seq_size
    blocks = kv_cache.shape[1]
    experts, _, _, ff = expert_in.shape
    qcols = q_weight.shape[1]
    vcols = qcols + 2 * HEAD_DIM
    owner = block_owners(block_count, placement)
    step = jnp.arange(8)
    column = jnp.where(step[None, :] < steps, owner[:, None] + step[None, :] * requests, -1)
    sel = column.reshape(-1)[:, None] == jnp.arange(rows)[None, :]
    same = owner[:, None] == owner[None, :]
    earlier = jnp.arange(blocks)[:, None] > jnp.arange(blocks)[None, :]
    leads = jnp.logical_not(jnp.any(same & earlier, axis=1))
    lead = sel & jnp.repeat(leads, 8)[:, None]
    penalty = jnp.where(same, 0.0, NEGATIVE).astype(F32).reshape(-1)
    alive = (block_live == 1).astype(F32)
    onehot = (routes[:, :, None] == jnp.arange(LANES)[None, None, :]).astype(F32)
    onehot = onehot.reshape(seq_size, rp, TOPK, LANES).transpose(0, 2, 1, 3)
    acols, ecols, bcols = vcols + LANES, qcols + LANES, 2 * ff + LANES
    ry = rows // ny
    vmem = pl.BlockSpec(memory_space=pltpu.VMEM)
    smem = pl.BlockSpec(memory_space=pltpu.SMEM)
    return pl.pallas_call(
        functools.partial(kernel, (ny, nz, nx, width * seq_size, steps)),
        out_shape=jax.ShapeDtypeStruct((width, rows), BF16),
        in_specs=[smem, smem] + [vmem] * 13,
        out_specs=vmem,
        scratch_shapes=[
            pltpu.VMEM((ny, ry, acols), BF16),
            pltpu.VMEM((ny, ry, acols), BF16),
            pltpu.VMEM((nz, rp, acols), BF16),
            pltpu.VMEM((nz, rp, acols), BF16),
            pltpu.VMEM((ny, nz, rp, vcols), BF16),
            pltpu.VMEM((ny, ry, ecols), BF16),
            pltpu.VMEM((ny, ry, ecols), BF16),
            pltpu.VMEM((nz, rp, ecols), BF16),
            pltpu.VMEM((nz, rp, ecols), BF16),
            pltpu.VMEM((ny, nz, rp, qcols), BF16),
            pltpu.VMEM((ny, TOPK * ry, bcols), BF16),
            pltpu.VMEM((ny, TOPK * ry, bcols), BF16),
            pltpu.VMEM((nz, TOPK, rp, bcols), BF16),
            pltpu.VMEM((nz, TOPK, rp, bcols), BF16),
            pltpu.VMEM((ny, nz, TOPK, rp, ff), BF16),
            pltpu.VMEM((width, rows), BF16),
            pltpu.VMEM((nx, width, rows), BF16),
            pltpu.VMEM((width, rows), BF16),
            pltpu.VMEM((nx, width, rows), BF16),
            pltpu.SemaphoreType.DMA((ny - 1,)),
            pltpu.SemaphoreType.DMA((nz - 1,)),
            pltpu.SemaphoreType.DMA((nx - 1,)),
            pltpu.SemaphoreType.DMA((6, ny - 1)),
            pltpu.SemaphoreType.DMA((6, nz - 1)),
            pltpu.SemaphoreType.DMA((2, nx - 1)),
        ],
        compiler_params=pltpu.CompilerParams(
            collective_id=0, has_side_effects=True, vmem_limit_bytes=60 * 1024 * 1024
        ),
    )(
        penalty,
        alive,
        tokens,
        norm_gains.T,
        q_weight,
        kv_weight.reshape(width, -1),
        out_weight,
        kv_cache,
        sel.astype(F32),
        lead.astype(F32),
        jnp.pad(router_weight, ((0, 0), (0, LANES - experts))),
        routes.T,
        onehot,
        expert_in,
        expert_out,
    )


def solution(mesh):
    return jax.shard_map(
        functools.partial(per_device, mesh.shape["exp"], mesh.shape["seq"]),
        mesh=mesh,
        in_specs=(
            P("seq", None),
            P(None, "seq"),
            P("seq", "exp"),
            P("seq", None, "exp"),
            P("seq", "exp"),
            P(None, "seq", None, "exp"),
            P(),
            P("seq"),
            P("seq"),
            P("seq", None),
            P(),
            P(None, None, "seq", "exp"),
            P(None, "seq", "exp"),
        ),
        out_specs=P("seq", None),
        check_vma=False,
    )
```

```python
import functools
import math

import jax
import jax.numpy as jnp
from jax import lax
from jax.experimental import pallas as pl
from jax.experimental.pallas import tpu as pltpu
from jax.sharding import PartitionSpec as P

HEAD_DIM = 128
TOPK = 2
LANES = 128
NEGATIVE = -1e30
EPSILON = 1e-05
MESH = pl.DeviceIdType.MESH
HIGHEST = lax.Precision.HIGHEST
FIRST = (((0,), (0,)), ((), ()))
LAST = (((1,), (1,)), ((), ()))
MIDDLE = (((1,), (0,)), ((), ()))
F32 = jnp.float32
BF16 = jnp.bfloat16


def dot(first, second, dims, precision=None):
    return lax.dot_general(
        first, second, dims, precision=precision, preferred_element_type=F32
    )


def ring_order(count):
    return sorted(range(1, count), key=lambda d: -min(d, count - d))


def kernel(
    cfg,
    count_ref,
    place_ref,
    live_ref,
    route_ref,
    tok_ref,
    gains_ref,
    qw_ref,
    kvw_ref,
    ow_ref,
    cache_ref,
    router_ref,
    routes_ref,
    ein_ref,
    eout_ref,
    out_ref,
    a_sy,
    a_ry,
    a_sz,
    a_rz,
    a_g,
    e_sy,
    e_ry,
    e_sz,
    e_rz,
    e_g,
    s_sy,
    s_ry,
    s_sz,
    s_rz,
    b_sy,
    b_ry,
    b_sz,
    b_rz,
    b_g,
    x_s,
    x_p,
    x_r,
    y_send,
    z_send,
    x_send,
    y_recv,
    z_recv,
    x_recv,
):
    ny, nz, nx, depth, steps = cfg
    width, rows = tok_ref.shape
    requests = count_ref.shape[0]
    ry = rows // ny
    rp = ry // nz
    heads = qw_ref.shape[1] // HEAD_DIM
    qcols = heads * HEAD_DIM
    kcols = qcols + HEAD_DIM
    vcols = kcols + HEAD_DIM
    blocks = cache_ref.shape[1]
    experts = ein_ref.shape[0]
    ff = ein_ref.shape[3]
    scale = 1.0 / math.sqrt(HEAD_DIM)
    seq = lax.axis_index("seq")
    e = lax.axis_index("exp")
    y = lax.div(seq, nz)
    z = lax.rem(seq, nz)
    chips = nx // 2
    chip = lax.div(e, 2)
    partner = e + 1 - 2 * lax.rem(e, 2)
    started = []

    def y_peer(d):
        return lax.rem(y + d, ny)

    def z_peer(d):
        return lax.rem(z + d, nz)

    def chip_peer(d):
        return lax.rem(e + 2 * d, nx)

    def push(src, dst, send_sem, recv_sem, device):
        copy = pltpu.make_async_remote_copy(
            src_ref=src,
            dst_ref=dst,
            send_sem=send_sem,
            recv_sem=recv_sem,
            device_id=device,
            device_id_type=MESH,
        )
        copy.start()
        started.append(copy)
        return copy

    def y_push(src, dst, d, phase):
        device = (y_peer(d) * nz + z, e)
        return push(src, dst, y_send.at[phase, d - 1], y_recv.at[phase, d - 1], device)

    def z_push(src, dst, d, phase):
        device = (y * nz + z_peer(d), e)
        return push(src, dst, z_send.at[phase, d - 1], z_recv.at[phase, d - 1], device)

    def arrive(copies):
        for copy in copies:
            copy.wait_recv()

    def y_exchange(send, recv, phase):
        return [y_push(send.at[y_peer(d)], recv.at[d - 1], d, phase) for d in ring_order(ny)]

    def z_exchange(send, recv, phase):
        return [z_push(send.at[z_peer(d)], recv.at[d - 1], d, phase) for d in ring_order(nz)]

    def z_gather(held, phase):
        return [z_push(held.at[y, z], held.at[y, z], d, phase) for d in ring_order(nz)]

    def y_gather(held, phase):
        return [y_push(held.at[y], held.at[y], d, phase) for d in ring_order(ny)]

    def gather(held, phase):
        arrive(z_gather(held, phase))
        arrive(y_gather(held, phase))

    def summed(own, recv, copies):
        total = own.astype(F32)
        arrive(copies)
        for slot in range(len(copies)):
            total = total + recv[slot].astype(F32)
        return total

    def x_reduce(part, phase):
        first, second = x_s.at[phase, 0], x_s.at[phase, 1]
        first[...] = part.astype(BF16)
        copy = push(
            first, x_p.at[phase], x_send.at[phase, 0], x_recv.at[phase, 0], (seq, partner)
        )
        copy.wait_recv()
        pair = (first[...].astype(F32) + x_p[phase].astype(F32)).astype(BF16)
        second[...] = pair
        x_r[phase, chip] = pair
        arrive(
            [
                push(
                    second,
                    x_r.at[phase, chip],
                    x_send.at[phase, d],
                    x_recv.at[phase, d],
                    (seq, chip_peer(d)),
                )
                for d in ring_order(chips)
            ]
        )
        total = x_r[phase, 0].astype(F32)
        for index in range(1, chips):
            total = total + x_r[phase, index].astype(F32)
        return total

    barrier = pltpu.get_barrier_semaphore()
    for d in ring_order(nz):
        pl.semaphore_signal(barrier, inc=1, device_id=(y * nz + z_peer(d), e), device_id_type=MESH)
    for d in range(1, ny):
        pl.semaphore_signal(barrier, inc=1, device_id=(y_peer(d) * nz + z, e), device_id_type=MESH)
    pl.semaphore_signal(barrier, inc=1, device_id=(seq, partner), device_id_type=MESH)
    for d in range(1, chips):
        pl.semaphore_signal(barrier, inc=1, device_id=(seq, chip_peer(d)), device_id_type=MESH)

    def iota(shape, axis):
        return lax.broadcasted_iota(jnp.int32, shape, axis)

    def lane_of(count):
        return iota((count, LANES), 1)

    def by_head(columns):
        count = columns[0].shape[0]
        lane = lax.rem(lane_of(count), heads)
        spread = jnp.broadcast_to(columns[0], (count, LANES))
        for h in range(1, heads):
            spread = jnp.where(lane == h, columns[h], spread)
        return spread

    def thirds(values):
        high = values.astype(BF16).astype(F32)
        rest = values - high
        middle = rest.astype(BF16).astype(F32)
        return high, middle, rest - middle

    def pack_stats(top, total):
        group = lax.div(lane_of(top.shape[0]), heads)
        high, middle, low = thirds(top)
        total_high = total.astype(BF16).astype(F32)
        packed = jnp.where(group == 0, high, total - total_high)
        packed = jnp.where(group == 1, middle, packed)
        packed = jnp.where(group == 2, low, packed)
        packed = jnp.where(group == 3, total_high, packed)
        return packed

    def stat(values, group, h):
        lane = qcols + group * heads + h
        return values[..., lane : lane + 1]

    def unpack(values, h):
        top = (stat(values, 0, h) + stat(values, 1, h)) + stat(values, 2, h)
        total = stat(values, 3, h) + stat(values, 4, h)
        return top, total, values[..., h * HEAD_DIM : (h + 1) * HEAD_DIM]

    def column(row):
        size = row.shape[1]
        on = iota((size, size), 0) == iota((size, size), 1)
        return jnp.sum(jnp.where(on, row, 0.0), axis=1, keepdims=True)

    tok = tok_ref[...].astype(F32)
    ones = jnp.ones((width, LANES), F32)
    normed = (tok * column(gains_ref[0:1, :])).astype(BF16)
    second_gain = column(gains_ref[1:2, :])
    q_part = dot(normed, qw_ref[...], FIRST)
    kv_weight = kvw_ref[...].astype(F32)
    k_part = dot(normed, kv_weight[:, 0, :].astype(BF16), FIRST)
    v_part = dot(normed, kv_weight[:, 1, :].astype(BF16), FIRST)
    squares = dot(tok * tok, ones, FIRST, HIGHEST)
    for part in range(ny):
        here = slice(part * ry, (part + 1) * ry)
        a_sy[part, :, 0:qcols] = q_part[here].astype(BF16)
        a_sy[part, :, qcols:kcols] = k_part[here].astype(BF16)
        a_sy[part, :, kcols:vcols] = v_part[here].astype(BF16)
        a_sy[part, :, vcols : vcols + LANES] = squares[here].astype(BF16)

    pl.semaphore_wait(barrier, (ny - 1) + (nz - 1) + chips)
    copies = y_exchange(a_sy, a_ry, 0)

    owners = []
    for p in range(blocks):
        place, start, owner = place_ref[p], 0, -1
        for r in range(requests):
            owner = owner + (place >= start).astype(jnp.int32)
            start = start + count_ref[r]
        owners.append(owner)
    same = [[(owners[p] == owners[q]).astype(jnp.int32) for q in range(blocks)] for p in range(blocks)]
    select, leads = [], []
    step = iota((8, rows), 0)
    wanted = iota((8, rows), 1)
    for p in range(blocks):
        chosen = (wanted == owners[p] + step * requests) & (step < steps)
        chosen = jnp.where(chosen, 1.0, 0.0)
        select.append(chosen)
        first = 1
        for q in range(p):
            first = first * (1 - same[p][q])
        leads.append(chosen * first.astype(F32) if p else chosen)
    select = jnp.concatenate(select, axis=0).astype(BF16)
    leads = jnp.concatenate(leads, axis=0).astype(BF16)

    part_sum = summed(a_sy[y], a_ry, copies)
    a_sz[...] = part_sum.reshape(nz, rp, part_sum.shape[1]).astype(BF16)
    copies = z_exchange(a_sz, a_rz, 0)
    arrive(copies)
    fresh = a_sz[z].astype(F32) + jnp.sum(a_rz[...].astype(F32), axis=0)
    attn_rms = lax.rsqrt(fresh[:, vcols : vcols + 1] / depth + EPSILON)
    own = (fresh[:, 0:vcols] * attn_rms).astype(BF16)
    a_g[y, z] = own
    gather(a_g, 1)
    fresh_rows = a_g[...].astype(F32).reshape(rows, vcols)[:, 0:qcols].astype(BF16)

    picked = dot(select, fresh_rows, MIDDLE)
    tops, totals, sums = [], [], []
    for p in range(blocks):
        here = slice(p * 8, (p + 1) * 8)
        block_query = jnp.concatenate(
            [picked[here, h * HEAD_DIM : (h + 1) * HEAD_DIM] for h in range(heads)], axis=0
        )
        scores = dot(block_query.astype(BF16), cache_ref[0, p], LAST) * scale
        top = jnp.max(scores, axis=1, keepdims=True)
        weights = jnp.exp(scores - top).astype(BF16)
        total = jnp.sum(weights.astype(F32), axis=1, keepdims=True)
        weighted = dot(weights, cache_ref[1, p], MIDDLE)
        alive = live_ref[p].astype(F32)
        top = by_head([top[h * 8 : (h + 1) * 8] for h in range(heads)])
        tops.append(top * alive + (1.0 - alive) * NEGATIVE)
        totals.append(by_head([total[h * 8 : (h + 1) * 8] for h in range(heads)]) * alive)
        sums.append(weighted * alive)
    joint, joint_sums = [], []
    for p in range(blocks):
        best = tops[p]
        for q in range(blocks):
            if q != p:
                apart = (1 - same[p][q]).astype(F32) * NEGATIVE
                best = jnp.maximum(best, tops[q] + apart)
        factor = jnp.exp(tops[p] - best)
        joint.append(best)
        joint_sums.append(
            jnp.concatenate(
                [sums[p][h * 8 : (h + 1) * 8] * factor[:, h : h + 1] for h in range(heads)]
                + [totals[p] * factor],
                axis=1,
            )
        )
    joint_sums = jnp.concatenate(joint_sums, axis=0)
    sums_high = joint_sums.astype(BF16)
    sums_low = (joint_sums - sums_high.astype(F32)).astype(BF16)
    local = dot(select, sums_high, FIRST) + dot(select, sums_low, FIRST)
    joint = jnp.concatenate(joint, axis=0)
    joint = jnp.where(lane_of(joint.shape[0]) < LANES // 2, joint, 1.0)
    local_top = sum(dot(leads, third.astype(BF16), FIRST) for third in reversed(thirds(joint)))
    present = local_top[:, LANES - 1 : LANES] > 0.5
    local_top = jnp.where(present, local_top, NEGATIVE)
    local_stats = pack_stats(local_top, local[:, qcols : qcols + LANES]).astype(BF16)
    for part in range(ny):
        here = slice(part * ry, (part + 1) * ry)
        e_sy[part, :, 0:qcols] = local[here, 0:qcols].astype(BF16)
        e_sy[part, :, qcols : qcols + LANES] = local_stats[here]
    copies = y_exchange(e_sy, e_ry, 2)

    own = own.astype(F32)
    new_rows = [a_g[s, z].astype(F32) for s in range(steps)]
    fresh_parts = []
    for h in range(heads):
        query = own[:, h * HEAD_DIM : (h + 1) * HEAD_DIM]
        scores = []
        for s in range(steps):
            score = jnp.sum(query * new_rows[s][:, qcols:kcols], axis=1, keepdims=True) * scale
            scores.append(jnp.where(y >= s, score, NEGATIVE))
        new_top = functools.reduce(jnp.maximum, scores)
        new_total, new_sum = 0.0, 0.0
        for s in range(steps):
            weight = jnp.where(y >= s, jnp.exp(scores[s] - new_top), 0.0)
            weight = weight.astype(BF16).astype(F32)
            new_total = new_total + weight
            new_sum = new_sum + weight * new_rows[s][:, kcols:vcols]
        fresh_parts.append((new_top, new_total, new_sum))

    arrive(copies)
    parts = [e_sy[y].astype(F32)] + [e_ry[slot].astype(F32) for slot in range(ny - 1)]
    tops, totals = [], []
    for h in range(heads):
        pieces = [unpack(values, h) for values in parts]
        top = functools.reduce(jnp.maximum, [piece[0] for piece in pieces])
        total, weighted = 0.0, 0.0
        for piece in pieces:
            factor = jnp.exp(piece[0] - top)
            total = total + factor * piece[1]
            weighted = weighted + factor * piece[2]
        tops.append(top)
        totals.append(total)
        e_sz[:, :, h * HEAD_DIM : (h + 1) * HEAD_DIM] = weighted.reshape(nz, rp, HEAD_DIM).astype(BF16)
    stats = pack_stats(by_head(tops), by_head(totals))
    e_sz[:, :, qcols : qcols + LANES] = stats.reshape(nz, rp, LANES).astype(BF16)
    copies = z_exchange(e_sz, e_rz, 2)
    arrive(copies)
    values = e_rz[...].astype(F32)
    mine = e_sz[z].astype(F32)
    attended = []
    for h in range(heads):
        tops, totals, sums = unpack(values, h)
        my_top, my_total, my_sum = unpack(mine, h)
        new_top, new_total, new_sum = fresh_parts[h]
        joined = jnp.maximum(jnp.maximum(jnp.max(tops, axis=0), my_top), new_top)
        factors = jnp.exp(tops - joined[None])
        my_factor = jnp.exp(my_top - joined)
        new_factor = jnp.exp(new_top - joined)
        total = jnp.sum(factors * totals, axis=0) + my_total * my_factor + new_total * new_factor
        weighted = jnp.sum(factors * sums, axis=0) + my_sum * my_factor + new_sum * new_factor
        attended.append(weighted / total)
    e_g[y, z] = jnp.concatenate(attended, axis=1).astype(BF16)
    gather(e_g, 3)
    attention = e_g[...].astype(F32).reshape(rows, qcols).astype(BF16)

    head_part = dot(ow_ref[...], attention, LAST)
    residual = tok + x_reduce(head_part, 0)

    hidden = (residual * second_gain).astype(BF16)
    hidden_float = hidden.astype(F32)
    router = jnp.concatenate(
        [router_ref[...].astype(F32), jnp.zeros((LANES - experts, width), F32)], axis=0
    ).astype(BF16)
    logits = dot(hidden, router, (((0,), (1,)), ((), ())))
    squares = dot(residual * residual, ones, FIRST, HIGHEST)
    stats = jnp.where(lane_of(rows) < experts, logits, squares).astype(BF16)
    for part in range(ny):
        s_sy[part] = stats[part * ry : (part + 1) * ry]
    stat_copies = y_exchange(s_sy, s_ry, 4)
    chunks = [(k, c) for k in range(TOPK) for c in range(2)]
    masked = [None] * TOPK
    y_copies, z_copies = [], []

    def pass_on(j):
        part_sum = summed(b_sy[j, y], b_ry.at[j], y_copies[j])
        b_sz[j] = part_sum.reshape(nz, rp, ff).astype(BF16)
        z_copies.append(z_exchange(b_sz.at[j], b_rz.at[j], 5 + j))

    for j, (k, c) in enumerate(chunks):
        if c == 0:
            masked = jnp.concatenate(
                [
                    jnp.where(routes_ref[k : k + 1, :] == expert, hidden_float, 0.0)
                    for expert in range(experts)
                ],
                axis=0,
            ).astype(BF16)
        product = dot(masked, ein_ref[:, c].reshape(experts * width, ff), FIRST)
        for part in range(ny):
            b_sy[j, part] = product[part * ry : (part + 1) * ry].astype(BF16)
        y_copies.append(y_exchange(b_sy.at[j], b_ry.at[j], 5 + j))
        if j == 0:
            part_sum = summed(s_sy[y], s_ry, stat_copies)
            s_sz[...] = part_sum.reshape(nz, rp, LANES).astype(BF16)
            stat_copies = z_exchange(s_sz, s_rz, 4)
        if j >= 2:
            pass_on(j - 2)
    pass_on(2)
    pass_on(3)
    arrive(stat_copies)
    stats = s_sz[z].astype(F32) + jnp.sum(s_rz[...].astype(F32), axis=0)
    moe_rms = lax.rsqrt(stats[:, LANES // 2 : LANES // 2 + 1] / depth + EPSILON)
    sigmoids = []
    for k in range(TOPK):
        wanted = jnp.full((rp, LANES), route_ref[k, seq * rp], jnp.int32)
        for row in range(1, rp):
            wanted = jnp.where(iota((rp, LANES), 0) == row, route_ref[k, seq * rp + row], wanted)
        logit = jnp.sum(jnp.where(lane_of(rp) == wanted, stats, 0.0), axis=1, keepdims=True) * moe_rms
        sigmoids.append(1.0 / (1.0 + jnp.exp(-logit)))
    z_held = []
    for k in range(TOPK):
        pair = []
        for c in range(2):
            j = 2 * k + c
            arrive(z_copies[j])
            pair.append((b_sz[j, z].astype(F32) + jnp.sum(b_rz[j].astype(F32), axis=0)) * moe_rms)
        active = pair[0] / (1.0 + jnp.exp(-pair[0])) * pair[1]
        b_g[k, y, z] = (active * (sigmoids[k] / (sigmoids[0] + sigmoids[1]))).astype(BF16)
        z_held.append(z_gather(b_g.at[k], 9 + k))
    y_held = []
    for k in range(TOPK):
        arrive(z_held[k])
        y_held.append(y_gather(b_g.at[k], 9 + k))
    expert_part = jnp.zeros(residual.shape, F32)
    for k in range(TOPK):
        arrive(y_held[k])
        active = b_g[k].astype(F32).reshape(rows, ff).astype(BF16)
        product = dot(eout_ref[...].reshape(experts * width, ff), active, LAST)
        for expert in range(experts):
            expert_part = expert_part + jnp.where(
                routes_ref[k : k + 1, :] == expert,
                product[expert * width : (expert + 1) * width],
                0.0,
            )
    out_ref[...] = (residual + x_reduce(expert_part, 1)).astype(BF16)
    for copy in started:
        copy.wait_send()


def per_device(
    nx,
    seq_size,
    tokens,
    norm_gains,
    q_weight,
    kv_weight,
    out_weight,
    kv_cache,
    block_count,
    placement,
    block_live,
    router_weight,
    routes,
    expert_in,
    expert_out,
):
    width, rows = tokens.shape
    steps = rows // block_count.shape[0]
    ny, nz = steps, seq_size // steps
    rp = rows // seq_size
    ff = expert_in.shape[3]
    qcols = q_weight.shape[1]
    vcols = qcols + 2 * HEAD_DIM
    acols, ecols = vcols + LANES, qcols + LANES
    ry = rows // ny
    chunks = 2 * TOPK
    phases = 7 + chunks
    vmem = pl.BlockSpec(memory_space=pltpu.VMEM)
    smem = pl.BlockSpec(memory_space=pltpu.SMEM)
    return pl.pallas_call(
        functools.partial(kernel, (ny, nz, nx, width * seq_size, steps)),
        out_shape=jax.ShapeDtypeStruct((width, rows), BF16),
        in_specs=[smem] * 4 + [vmem] * 10,
        out_specs=vmem,
        scratch_shapes=[
            pltpu.VMEM((ny, ry, acols), BF16),
            pltpu.VMEM((ny - 1, ry, acols), BF16),
            pltpu.VMEM((nz, rp, acols), BF16),
            pltpu.VMEM((nz - 1, rp, acols), BF16),
            pltpu.VMEM((ny, nz, rp, vcols), BF16),
            pltpu.VMEM((ny, ry, ecols), BF16),
            pltpu.VMEM((ny - 1, ry, ecols), BF16),
            pltpu.VMEM((nz, rp, ecols), BF16),
            pltpu.VMEM((nz - 1, rp, ecols), BF16),
            pltpu.VMEM((ny, nz, rp, qcols), BF16),
            pltpu.VMEM((ny, ry, LANES), BF16),
            pltpu.VMEM((ny - 1, ry, LANES), BF16),
            pltpu.VMEM((nz, rp, LANES), BF16),
            pltpu.VMEM((nz - 1, rp, LANES), BF16),
            pltpu.VMEM((chunks, ny, ry, ff), BF16),
            pltpu.VMEM((chunks, ny - 1, ry, ff), BF16),
            pltpu.VMEM((chunks, nz, rp, ff), BF16),
            pltpu.VMEM((chunks, nz - 1, rp, ff), BF16),
            pltpu.VMEM((TOPK, ny, nz, rp, ff), BF16),
            pltpu.VMEM((2, 2, width, rows), BF16),
            pltpu.VMEM((2, width, rows), BF16),
            pltpu.VMEM((2, nx // 2, width, rows), BF16),
            pltpu.SemaphoreType.DMA((phases, ny - 1)),
            pltpu.SemaphoreType.DMA((phases, nz - 1)),
            pltpu.SemaphoreType.DMA((2, nx // 2)),
            pltpu.SemaphoreType.DMA((phases, ny - 1)),
            pltpu.SemaphoreType.DMA((phases, nz - 1)),
            pltpu.SemaphoreType.DMA((2, nx // 2)),
        ],
        compiler_params=pltpu.CompilerParams(
            collective_id=0, has_side_effects=True, vmem_limit_bytes=60 * 1024 * 1024
        ),
    )(
        block_count,
        placement,
        block_live,
        routes.T,
        tokens,
        norm_gains,
        q_weight,
        kv_weight,
        out_weight,
        kv_cache,
        router_weight.T,
        routes.T,
        expert_in,
        expert_out,
    )


def solution(mesh):
    return jax.shard_map(
        functools.partial(per_device, mesh.shape["exp"], mesh.shape["seq"]),
        mesh=mesh,
        in_specs=(
            P("seq", None),
            P(None, "seq"),
            P("seq", "exp"),
            P("seq", None, "exp"),
            P("seq", "exp"),
            P(None, "seq", None, "exp"),
            P(),
            P("seq"),
            P("seq"),
            P("seq", None),
            P(),
            P(None, None, "seq", "exp"),
            P(None, "seq", "exp"),
        ),
        out_specs=P("seq", None),
        check_vma=False,
    )
```

```python
import functools
import math

import jax
import jax.numpy as jnp
from jax import lax
from jax.experimental import pallas as pl
from jax.experimental.pallas import tpu as pltpu
from jax.sharding import PartitionSpec as P

HEAD_DIM = 128
TOPK = 2
LANES = 128
NEGATIVE = -1e30
EPSILON = 1e-05
MESH = pl.DeviceIdType.MESH
HIGHEST = lax.Precision.HIGHEST
FIRST = (((0,), (0,)), ((), ()))
LAST = (((1,), (1,)), ((), ()))
MIDDLE = (((1,), (0,)), ((), ()))
F32 = jnp.float32
BF16 = jnp.bfloat16


def dot(first, second, dims, precision=None):
    return lax.dot_general(
        first, second, dims, precision=precision, preferred_element_type=F32
    )


def ring_order(count):
    return sorted(range(1, count), key=lambda d: -min(d, count - d))


def kernel(
    cfg,
    count_ref,
    place_ref,
    live_ref,
    route_ref,
    tok_ref,
    gains_ref,
    qw_ref,
    kvw_ref,
    ow_ref,
    cache_hbm,
    router_ref,
    routes_ref,
    ein_hbm,
    eout_hbm,
    out_ref,
    a_sy,
    a_ry,
    a_sz,
    a_rz,
    a_g,
    e_sy,
    e_ry,
    e_sz,
    e_rz,
    e_g,
    s_sy,
    s_ry,
    s_sz,
    s_rz,
    b_sy,
    b_ry,
    b_sz,
    b_rz,
    b_g,
    x_s,
    x_p,
    x_r,
    y_send,
    z_send,
    x_send,
    y_recv,
    z_recv,
    x_recv,
    cache_ref,
    ein_ref,
    eout_ref,
    load_sem,
):
    ny, nz, nx, depth, steps = cfg
    width, rows = tok_ref.shape
    requests = count_ref.shape[0]
    ry = rows // ny
    rp = ry // nz
    heads = qw_ref.shape[1] // HEAD_DIM
    qcols = heads * HEAD_DIM
    kcols = qcols + HEAD_DIM
    vcols = kcols + HEAD_DIM
    blocks = cache_ref.shape[1]
    experts = ein_ref.shape[0]
    ff = ein_ref.shape[3]
    scale = 1.0 / math.sqrt(HEAD_DIM)
    seq = lax.axis_index("seq")
    e = lax.axis_index("exp")
    y = lax.div(seq, nz)
    z = lax.rem(seq, nz)
    chips = nx // 2
    chip = lax.div(e, 2)
    partner = e + 1 - 2 * lax.rem(e, 2)
    started = []

    def y_peer(d):
        return lax.rem(y + d, ny)

    def z_peer(d):
        return lax.rem(z + d, nz)

    def chip_peer(d):
        return lax.rem(e + 2 * d, nx)

    def push(src, dst, send_sem, recv_sem, device):
        copy = pltpu.make_async_remote_copy(
            src_ref=src,
            dst_ref=dst,
            send_sem=send_sem,
            recv_sem=recv_sem,
            device_id=device,
            device_id_type=MESH,
        )
        copy.start()
        started.append(copy)
        return copy

    def y_push(src, dst, d, phase):
        device = (y_peer(d) * nz + z, e)
        return push(src, dst, y_send.at[phase, d - 1], y_recv.at[phase, d - 1], device)

    def z_push(src, dst, d, phase):
        device = (y * nz + z_peer(d), e)
        return push(src, dst, z_send.at[phase, d - 1], z_recv.at[phase, d - 1], device)

    def arrive(copies):
        for copy in copies:
            copy.wait_recv()

    def y_exchange(send, recv, phase):
        return [y_push(send.at[y_peer(d)], recv.at[d - 1], d, phase) for d in ring_order(ny)]

    def z_exchange(send, recv, phase):
        return [z_push(send.at[z_peer(d)], recv.at[d - 1], d, phase) for d in ring_order(nz)]

    def y_copy(src, d, phase):
        return pltpu.make_async_remote_copy(
            src_ref=src,
            dst_ref=src,
            send_sem=y_send.at[phase, d - 1],
            recv_sem=y_recv.at[phase, d - 1],
            device_id=(y_peer(d) * nz + z, e),
            device_id_type=MESH,
        )

    def forward(held, slot, phase):
        for d in ring_order(ny):
            y_copy(held.at[y, slot], d, phase).start()

    def z_gather(held, phase):
        copies = [z_push(held.at[y, z], held.at[y, z], d, phase) for d in ring_order(nz)]
        forward(held, z, phase)
        return copies

    def y_gather(held, phase, copies):
        for d, copy in reversed(list(zip(ring_order(nz), copies))):
            copy.wait_recv()
            forward(held, lax.rem(z + nz - d, nz), phase)
        whole = [y_copy(held.at[y], d, phase) for d in ring_order(ny)]
        started.extend(whole)
        return whole

    def gather(held, phase):
        arrive(y_gather(held, phase, z_gather(held, phase)))

    def summed(own, recv, copies):
        total = own.astype(F32)
        arrive(copies)
        for slot in range(len(copies)):
            total = total + recv[slot].astype(F32)
        return total

    def x_reduce(part, phase):
        first, second = x_s.at[phase, 0], x_s.at[phase, 1]
        first[...] = part.astype(BF16)
        copy = push(
            first, x_p.at[phase], x_send.at[phase, 0], x_recv.at[phase, 0], (seq, partner)
        )
        copy.wait_recv()
        pair = (first[...].astype(F32) + x_p[phase].astype(F32)).astype(BF16)
        second[...] = pair
        x_r[phase, chip] = pair
        arrive(
            [
                push(
                    second,
                    x_r.at[phase, chip],
                    x_send.at[phase, d],
                    x_recv.at[phase, d],
                    (seq, chip_peer(d)),
                )
                for d in ring_order(chips)
            ]
        )
        total = x_r[phase, 0].astype(F32)
        for index in range(1, chips):
            total = total + x_r[phase, index].astype(F32)
        return total

    barrier = pltpu.get_barrier_semaphore()
    for d in ring_order(nz):
        pl.semaphore_signal(barrier, inc=1, device_id=(y * nz + z_peer(d), e), device_id_type=MESH)
    for d in range(1, ny):
        pl.semaphore_signal(barrier, inc=1, device_id=(y_peer(d) * nz + z, e), device_id_type=MESH)
    pl.semaphore_signal(barrier, inc=1, device_id=(seq, partner), device_id_type=MESH)
    for d in range(1, chips):
        pl.semaphore_signal(barrier, inc=1, device_id=(seq, chip_peer(d)), device_id_type=MESH)

    def iota(shape, axis):
        return lax.broadcasted_iota(jnp.int32, shape, axis)

    def lane_of(count):
        return iota((count, LANES), 1)

    def by_head(columns):
        count = columns[0].shape[0]
        lane = lax.rem(lane_of(count), heads)
        spread = jnp.broadcast_to(columns[0], (count, LANES))
        for h in range(1, heads):
            spread = jnp.where(lane == h, columns[h], spread)
        return spread

    def thirds(values):
        high = values.astype(BF16).astype(F32)
        rest = values - high
        middle = rest.astype(BF16).astype(F32)
        return high, middle, rest - middle

    def pack_stats(top, total):
        group = lax.div(lane_of(top.shape[0]), heads)
        high, middle, low = thirds(top)
        total_high = total.astype(BF16).astype(F32)
        packed = jnp.where(group == 0, high, total - total_high)
        packed = jnp.where(group == 1, middle, packed)
        packed = jnp.where(group == 2, low, packed)
        packed = jnp.where(group == 3, total_high, packed)
        return packed

    def stat(values, group, h):
        lane = qcols + group * heads + h
        return values[..., lane : lane + 1]

    def unpack(values, h):
        top = (stat(values, 0, h) + stat(values, 1, h)) + stat(values, 2, h)
        total = stat(values, 3, h) + stat(values, 4, h)
        return top, total, values[..., h * HEAD_DIM : (h + 1) * HEAD_DIM]

    def column(row):
        size = row.shape[1]
        on = iota((size, size), 0) == iota((size, size), 1)
        return jnp.sum(jnp.where(on, row, 0.0), axis=1, keepdims=True)

    loads = [
        pltpu.make_async_copy(cache_hbm, cache_ref, load_sem.at[0]),
        pltpu.make_async_copy(ein_hbm, ein_ref, load_sem.at[1]),
        pltpu.make_async_copy(eout_hbm, eout_ref, load_sem.at[2]),
    ]
    for load in loads:
        load.start()

    tok = tok_ref[...].astype(F32)
    ones = jnp.ones((width, LANES), F32)
    normed = (tok * column(gains_ref[0:1, :])).astype(BF16)
    second_gain = column(gains_ref[1:2, :])
    q_part = dot(normed, qw_ref[...], FIRST)
    kv_weight = kvw_ref[...].astype(F32)
    k_part = dot(normed, kv_weight[:, 0, :].astype(BF16), FIRST)
    v_part = dot(normed, kv_weight[:, 1, :].astype(BF16), FIRST)
    squares = dot(tok * tok, ones, FIRST, HIGHEST)
    for part in range(ny):
        here = slice(part * ry, (part + 1) * ry)
        a_sy[part, :, 0:qcols] = q_part[here].astype(BF16)
        a_sy[part, :, qcols:kcols] = k_part[here].astype(BF16)
        a_sy[part, :, kcols:vcols] = v_part[here].astype(BF16)
        a_sy[part, :, vcols : vcols + LANES] = squares[here].astype(BF16)

    pl.semaphore_wait(barrier, (ny - 1) + (nz - 1) + chips)
    copies = y_exchange(a_sy, a_ry, 0)

    owners = []
    for p in range(blocks):
        place, start, owner = place_ref[p], 0, -1
        for r in range(requests):
            owner = owner + (place >= start).astype(jnp.int32)
            start = start + count_ref[r]
        owners.append(owner)
    same = [[(owners[p] == owners[q]).astype(jnp.int32) for q in range(blocks)] for p in range(blocks)]
    select, leads = [], []
    step = iota((8, rows), 0)
    wanted = iota((8, rows), 1)
    for p in range(blocks):
        chosen = (wanted == owners[p] + step * requests) & (step < steps)
        chosen = jnp.where(chosen, 1.0, 0.0)
        select.append(chosen)
        first = 1
        for q in range(p):
            first = first * (1 - same[p][q])
        leads.append(chosen * first.astype(F32) if p else chosen)
    select = jnp.concatenate(select, axis=0).astype(BF16)
    leads = jnp.concatenate(leads, axis=0).astype(BF16)

    part_sum = summed(a_sy[y], a_ry, copies)
    a_sz[...] = part_sum.reshape(nz, rp, part_sum.shape[1]).astype(BF16)
    copies = z_exchange(a_sz, a_rz, 0)
    arrive(copies)
    fresh = a_sz[z].astype(F32) + jnp.sum(a_rz[...].astype(F32), axis=0)
    attn_rms = lax.rsqrt(fresh[:, vcols : vcols + 1] / depth + EPSILON)
    own = (fresh[:, 0:vcols] * attn_rms).astype(BF16)
    a_g[y, z] = own
    gather(a_g, 1)
    fresh_rows = a_g[...].astype(F32).reshape(rows, vcols)[:, 0:qcols].astype(BF16)

    picked = dot(select, fresh_rows, MIDDLE)
    loads[0].wait()
    tops, totals, sums = [], [], []
    for p in range(blocks):
        here = slice(p * 8, (p + 1) * 8)
        block_query = jnp.concatenate(
            [picked[here, h * HEAD_DIM : (h + 1) * HEAD_DIM] for h in range(heads)], axis=0
        )
        scores = dot(block_query.astype(BF16), cache_ref[0, p], LAST) * scale
        top = jnp.max(scores, axis=1, keepdims=True)
        weights = jnp.exp(scores - top).astype(BF16)
        total = jnp.sum(weights.astype(F32), axis=1, keepdims=True)
        weighted = dot(weights, cache_ref[1, p], MIDDLE)
        alive = live_ref[p].astype(F32)
        top = by_head([top[h * 8 : (h + 1) * 8] for h in range(heads)])
        tops.append(top * alive + (1.0 - alive) * NEGATIVE)
        totals.append(by_head([total[h * 8 : (h + 1) * 8] for h in range(heads)]) * alive)
        sums.append(weighted * alive)
    joint, joint_sums = [], []
    for p in range(blocks):
        best = tops[p]
        for q in range(blocks):
            if q != p:
                apart = (1 - same[p][q]).astype(F32) * NEGATIVE
                best = jnp.maximum(best, tops[q] + apart)
        factor = jnp.exp(tops[p] - best)
        joint.append(best)
        joint_sums.append(
            jnp.concatenate(
                [sums[p][h * 8 : (h + 1) * 8] * factor[:, h : h + 1] for h in range(heads)]
                + [totals[p] * factor],
                axis=1,
            )
        )
    joint_sums = jnp.concatenate(joint_sums, axis=0)
    sums_high = joint_sums.astype(BF16)
    sums_low = (joint_sums - sums_high.astype(F32)).astype(BF16)
    local = dot(select, sums_high, FIRST) + dot(select, sums_low, FIRST)
    joint = jnp.concatenate(joint, axis=0)
    joint = jnp.where(lane_of(joint.shape[0]) < LANES // 2, joint, 1.0)
    local_top = sum(dot(leads, third.astype(BF16), FIRST) for third in reversed(thirds(joint)))
    present = local_top[:, LANES - 1 : LANES] > 0.5
    local_top = jnp.where(present, local_top, NEGATIVE)
    local_stats = pack_stats(local_top, local[:, qcols : qcols + LANES]).astype(BF16)
    for part in range(ny):
        here = slice(part * ry, (part + 1) * ry)
        e_sy[part, :, 0:qcols] = local[here, 0:qcols].astype(BF16)
        e_sy[part, :, qcols : qcols + LANES] = local_stats[here]
    copies = y_exchange(e_sy, e_ry, 2)

    own = own.astype(F32)
    new_rows = [a_g[s, z].astype(F32) for s in range(steps)]
    fresh_parts = []
    for h in range(heads):
        query = own[:, h * HEAD_DIM : (h + 1) * HEAD_DIM]
        scores = []
        for s in range(steps):
            score = jnp.sum(query * new_rows[s][:, qcols:kcols], axis=1, keepdims=True) * scale
            scores.append(jnp.where(y >= s, score, NEGATIVE))
        new_top = functools.reduce(jnp.maximum, scores)
        new_total, new_sum = 0.0, 0.0
        for s in range(steps):
            weight = jnp.where(y >= s, jnp.exp(scores[s] - new_top), 0.0)
            weight = weight.astype(BF16).astype(F32)
            new_total = new_total + weight
            new_sum = new_sum + weight * new_rows[s][:, kcols:vcols]
        fresh_parts.append((new_top, new_total, new_sum))

    arrive(copies)
    parts = [e_sy[y].astype(F32)] + [e_ry[slot].astype(F32) for slot in range(ny - 1)]
    tops, totals = [], []
    for h in range(heads):
        pieces = [unpack(values, h) for values in parts]
        top = functools.reduce(jnp.maximum, [piece[0] for piece in pieces])
        total, weighted = 0.0, 0.0
        for piece in pieces:
            factor = jnp.exp(piece[0] - top)
            total = total + factor * piece[1]
            weighted = weighted + factor * piece[2]
        tops.append(top)
        totals.append(total)
        e_sz[:, :, h * HEAD_DIM : (h + 1) * HEAD_DIM] = weighted.reshape(nz, rp, HEAD_DIM).astype(BF16)
    stats = pack_stats(by_head(tops), by_head(totals))
    e_sz[:, :, qcols : qcols + LANES] = stats.reshape(nz, rp, LANES).astype(BF16)
    copies = z_exchange(e_sz, e_rz, 2)
    arrive(copies)
    values = e_rz[...].astype(F32)
    mine = e_sz[z].astype(F32)
    attended = []
    for h in range(heads):
        tops, totals, sums = unpack(values, h)
        my_top, my_total, my_sum = unpack(mine, h)
        new_top, new_total, new_sum = fresh_parts[h]
        joined = jnp.maximum(jnp.maximum(jnp.max(tops, axis=0), my_top), new_top)
        factors = jnp.exp(tops - joined[None])
        my_factor = jnp.exp(my_top - joined)
        new_factor = jnp.exp(new_top - joined)
        total = jnp.sum(factors * totals, axis=0) + my_total * my_factor + new_total * new_factor
        weighted = jnp.sum(factors * sums, axis=0) + my_sum * my_factor + new_sum * new_factor
        attended.append(weighted / total)
    e_g[y, z] = jnp.concatenate(attended, axis=1).astype(BF16)
    gather(e_g, 3)
    attention = e_g[...].astype(F32).reshape(rows, qcols).astype(BF16)

    head_part = dot(ow_ref[...], attention, LAST)
    residual = tok + x_reduce(head_part, 0)

    hidden = (residual * second_gain).astype(BF16)
    hidden_float = hidden.astype(F32)
    router = jnp.concatenate(
        [router_ref[...].astype(F32), jnp.zeros((LANES - experts, width), F32)], axis=0
    ).astype(BF16)
    logits = dot(hidden, router, (((0,), (1,)), ((), ())))
    squares = dot(residual * residual, ones, FIRST, HIGHEST)
    stats = jnp.where(lane_of(rows) < experts, logits, squares).astype(BF16)
    for part in range(ny):
        s_sy[part] = stats[part * ry : (part + 1) * ry]
    stat_copies = y_exchange(s_sy, s_ry, 4)
    loads[1].wait()
    chunks = [(k, c) for k in range(TOPK) for c in range(2)]
    masked = [None] * TOPK
    y_copies, z_copies = [], []

    def pass_on(j):
        part_sum = summed(b_sy[j, y], b_ry.at[j], y_copies[j])
        b_sz[j] = part_sum.reshape(nz, rp, ff).astype(BF16)
        z_copies.append(z_exchange(b_sz.at[j], b_rz.at[j], 5 + j))

    for j, (k, c) in enumerate(chunks):
        if c == 0:
            masked = jnp.concatenate(
                [
                    jnp.where(routes_ref[k : k + 1, :] == expert, hidden_float, 0.0)
                    for expert in range(experts)
                ],
                axis=0,
            ).astype(BF16)
        product = dot(masked, ein_ref[:, c].reshape(experts * width, ff), FIRST)
        for part in range(ny):
            b_sy[j, part] = product[part * ry : (part + 1) * ry].astype(BF16)
        y_copies.append(y_exchange(b_sy.at[j], b_ry.at[j], 5 + j))
        if j == 0:
            part_sum = summed(s_sy[y], s_ry, stat_copies)
            s_sz[...] = part_sum.reshape(nz, rp, LANES).astype(BF16)
            stat_copies = z_exchange(s_sz, s_rz, 4)
        if j >= 2:
            pass_on(j - 2)
    pass_on(2)
    pass_on(3)
    arrive(stat_copies)
    stats = s_sz[z].astype(F32) + jnp.sum(s_rz[...].astype(F32), axis=0)
    moe_rms = lax.rsqrt(stats[:, LANES // 2 : LANES // 2 + 1] / depth + EPSILON)
    sigmoids = []
    for k in range(TOPK):
        wanted = jnp.full((rp, LANES), route_ref[k, seq * rp], jnp.int32)
        for row in range(1, rp):
            wanted = jnp.where(iota((rp, LANES), 0) == row, route_ref[k, seq * rp + row], wanted)
        logit = jnp.sum(jnp.where(lane_of(rp) == wanted, stats, 0.0), axis=1, keepdims=True) * moe_rms
        sigmoids.append(1.0 / (1.0 + jnp.exp(-logit)))
    z_held = []
    for k in range(TOPK):
        pair = []
        for c in range(2):
            j = 2 * k + c
            arrive(z_copies[j])
            pair.append((b_sz[j, z].astype(F32) + jnp.sum(b_rz[j].astype(F32), axis=0)) * moe_rms)
        active = pair[0] / (1.0 + jnp.exp(-pair[0])) * pair[1]
        b_g[k, y, z] = (active * (sigmoids[k] / (sigmoids[0] + sigmoids[1]))).astype(BF16)
        z_held.append(z_gather(b_g.at[k], 9 + k))
    y_held = []
    for k in range(TOPK):
        y_held.append(y_gather(b_g.at[k], 9 + k, z_held[k]))
    loads[2].wait()
    expert_part = jnp.zeros(residual.shape, F32)
    for k in range(TOPK):
        arrive(y_held[k])
        active = b_g[k].astype(F32).reshape(rows, ff).astype(BF16)
        product = dot(eout_ref[...].reshape(experts * width, ff), active, LAST)
        for expert in range(experts):
            expert_part = expert_part + jnp.where(
                routes_ref[k : k + 1, :] == expert,
                product[expert * width : (expert + 1) * width],
                0.0,
            )
    out_ref[...] = (residual + x_reduce(expert_part, 1)).astype(BF16)
    for copy in started:
        copy.wait_send()


def per_device(
    nx,
    seq_size,
    tokens,
    norm_gains,
    q_weight,
    kv_weight,
    out_weight,
    kv_cache,
    block_count,
    placement,
    block_live,
    router_weight,
    routes,
    expert_in,
    expert_out,
):
    width, rows = tokens.shape
    steps = rows // block_count.shape[0]
    ny, nz = steps, seq_size // steps
    rp = rows // seq_size
    ff = expert_in.shape[3]
    qcols = q_weight.shape[1]
    vcols = qcols + 2 * HEAD_DIM
    acols, ecols = vcols + LANES, qcols + LANES
    ry = rows // ny
    chunks = 2 * TOPK
    phases = 7 + chunks
    vmem = pl.BlockSpec(memory_space=pltpu.VMEM)
    smem = pl.BlockSpec(memory_space=pltpu.SMEM)
    held = pl.BlockSpec(memory_space=pl.ANY)
    return pl.pallas_call(
        functools.partial(kernel, (ny, nz, nx, width * seq_size, steps)),
        out_shape=jax.ShapeDtypeStruct((width, rows), BF16),
        in_specs=[smem] * 4 + [vmem] * 5 + [held, vmem, vmem, held, held],
        out_specs=vmem,
        scratch_shapes=[
            pltpu.VMEM((ny, ry, acols), BF16),
            pltpu.VMEM((ny - 1, ry, acols), BF16),
            pltpu.VMEM((nz, rp, acols), BF16),
            pltpu.VMEM((nz - 1, rp, acols), BF16),
            pltpu.VMEM((ny, nz, rp, vcols), BF16),
            pltpu.VMEM((ny, ry, ecols), BF16),
            pltpu.VMEM((ny - 1, ry, ecols), BF16),
            pltpu.VMEM((nz, rp, ecols), BF16),
            pltpu.VMEM((nz - 1, rp, ecols), BF16),
            pltpu.VMEM((ny, nz, rp, qcols), BF16),
            pltpu.VMEM((ny, ry, LANES), BF16),
            pltpu.VMEM((ny - 1, ry, LANES), BF16),
            pltpu.VMEM((nz, rp, LANES), BF16),
            pltpu.VMEM((nz - 1, rp, LANES), BF16),
            pltpu.VMEM((chunks, ny, ry, ff), BF16),
            pltpu.VMEM((chunks, ny - 1, ry, ff), BF16),
            pltpu.VMEM((chunks, nz, rp, ff), BF16),
            pltpu.VMEM((chunks, nz - 1, rp, ff), BF16),
            pltpu.VMEM((TOPK, ny, nz, rp, ff), BF16),
            pltpu.VMEM((2, 2, width, rows), BF16),
            pltpu.VMEM((2, width, rows), BF16),
            pltpu.VMEM((2, nx // 2, width, rows), BF16),
            pltpu.SemaphoreType.DMA((phases, ny - 1)),
            pltpu.SemaphoreType.DMA((phases, nz - 1)),
            pltpu.SemaphoreType.DMA((2, nx // 2)),
            pltpu.SemaphoreType.DMA((phases, ny - 1)),
            pltpu.SemaphoreType.DMA((phases, nz - 1)),
            pltpu.SemaphoreType.DMA((2, nx // 2)),
            pltpu.VMEM(kv_cache.shape, BF16),
            pltpu.VMEM(expert_in.shape, BF16),
            pltpu.VMEM(expert_out.shape, BF16),
            pltpu.SemaphoreType.DMA((3,)),
        ],
        compiler_params=pltpu.CompilerParams(
            collective_id=0, has_side_effects=True, vmem_limit_bytes=60 * 1024 * 1024
        ),
    )(
        block_count,
        placement,
        block_live,
        routes.T,
        tokens,
        norm_gains,
        q_weight,
        kv_weight,
        out_weight,
        kv_cache,
        router_weight.T,
        routes.T,
        expert_in,
        expert_out,
    )


def solution(mesh):
    return jax.shard_map(
        functools.partial(per_device, mesh.shape["exp"], mesh.shape["seq"]),
        mesh=mesh,
        in_specs=(
            P("seq", None),
            P(None, "seq"),
            P("seq", "exp"),
            P("seq", None, "exp"),
            P("seq", "exp"),
            P(None, "seq", None, "exp"),
            P(),
            P("seq"),
            P("seq"),
            P("seq", None),
            P(),
            P(None, None, "seq", "exp"),
            P(None, "seq", "exp"),
        ),
        out_specs=P("seq", None),
        check_vma=False,
    )
```

```python
import functools
import math

import jax
import jax.numpy as jnp
from jax import lax
from jax.experimental import pallas as pl
from jax.experimental.pallas import tpu as pltpu
from jax.sharding import PartitionSpec as P

HEAD_DIM = 128
TOPK = 2
LANES = 128
NEGATIVE = -1e30
EPSILON = 1e-05
MESH = pl.DeviceIdType.MESH
HIGHEST = lax.Precision.HIGHEST
FIRST = (((0,), (0,)), ((), ()))
LAST = (((1,), (1,)), ((), ()))
MIDDLE = (((1,), (0,)), ((), ()))
F32 = jnp.float32
BF16 = jnp.bfloat16


def dot(first, second, dims, precision=None):
    return lax.dot_general(
        first, second, dims, precision=precision, preferred_element_type=F32
    )


def ring_order(count):
    return sorted(range(1, count), key=lambda d: -min(d, count - d))


def kernel(
    cfg,
    count_ref,
    place_ref,
    live_ref,
    route_ref,
    tok_ref,
    gains_ref,
    qw_ref,
    kvw_ref,
    ow_ref,
    cache_hbm,
    router_ref,
    routes_ref,
    ein_hbm,
    eout_hbm,
    out_ref,
    a_sy,
    a_ry,
    a_sz,
    a_rz,
    a_g,
    e_sy,
    e_ry,
    e_sz,
    e_rz,
    e_g,
    s_sy,
    s_ry,
    s_sz,
    s_rz,
    b_sy,
    b_ry,
    b_sz,
    b_rz,
    b_g,
    x_s,
    x_p,
    x_r,
    y_send,
    z_send,
    x_send,
    y_recv,
    z_recv,
    x_recv,
    cache_ref,
    ein_ref,
    eout_ref,
    load_sem,
):
    ny, nz, nx, depth, steps = cfg
    width, rows = tok_ref.shape
    requests = count_ref.shape[0]
    ry = rows // ny
    rp = ry // nz
    heads = qw_ref.shape[1] // HEAD_DIM
    qcols = heads * HEAD_DIM
    kcols = qcols + HEAD_DIM
    vcols = kcols + HEAD_DIM
    blocks = cache_ref.shape[1]
    experts = ein_ref.shape[0]
    ff = ein_ref.shape[3]
    scale = 1.0 / math.sqrt(HEAD_DIM)
    seq = lax.axis_index("seq")
    e = lax.axis_index("exp")
    y = lax.div(seq, nz)
    z = lax.rem(seq, nz)
    chips = nx // 2
    chip = lax.div(e, 2)
    partner = e + 1 - 2 * lax.rem(e, 2)
    started = []

    def y_peer(d):
        return lax.rem(y + d, ny)

    def z_peer(d):
        return lax.rem(z + d, nz)

    def chip_peer(d):
        return lax.rem(e + 2 * d, nx)

    def push(src, dst, send_sem, recv_sem, device):
        copy = pltpu.make_async_remote_copy(
            src_ref=src,
            dst_ref=dst,
            send_sem=send_sem,
            recv_sem=recv_sem,
            device_id=device,
            device_id_type=MESH,
        )
        copy.start()
        started.append(copy)
        return copy

    def y_push(src, dst, d, phase):
        device = (y_peer(d) * nz + z, e)
        return push(src, dst, y_send.at[phase, d - 1], y_recv.at[phase, d - 1], device)

    def z_push(src, dst, d, phase):
        device = (y * nz + z_peer(d), e)
        return push(src, dst, z_send.at[phase, d - 1], z_recv.at[phase, d - 1], device)

    def arrive(copies):
        for copy in copies:
            copy.wait_recv()

    def y_exchange(send, recv, phase):
        return [y_push(send.at[y_peer(d)], recv.at[d - 1], d, phase) for d in ring_order(ny)]

    def z_exchange(send, recv, phase):
        return [z_push(send.at[z_peer(d)], recv.at[d - 1], d, phase) for d in ring_order(nz)]

    def y_copy(src, d, phase):
        return pltpu.make_async_remote_copy(
            src_ref=src,
            dst_ref=src,
            send_sem=y_send.at[phase, d - 1],
            recv_sem=y_recv.at[phase, d - 1],
            device_id=(y_peer(d) * nz + z, e),
            device_id_type=MESH,
        )

    def forward(held, slot, phase):
        for d in ring_order(ny):
            y_copy(held.at[y, slot], d, phase).start()

    def z_gather(held, phase):
        copies = [z_push(held.at[y, z], held.at[y, z], d, phase) for d in ring_order(nz)]
        forward(held, z, phase)
        return copies

    def y_gather(held, phase, copies):
        for d, copy in reversed(list(zip(ring_order(nz), copies))):
            copy.wait_recv()
            forward(held, lax.rem(z + nz - d, nz), phase)
        whole = [y_copy(held.at[y], d, phase) for d in ring_order(ny)]
        started.extend(whole)
        return whole

    def gather(held, phase):
        arrive(y_gather(held, phase, z_gather(held, phase)))

    def summed(own, recv, copies):
        total = own.astype(F32)
        arrive(copies)
        for slot in range(len(copies)):
            total = total + recv[slot].astype(F32)
        return total

    def x_reduce(part, phase):
        first, second = x_s.at[phase, 0], x_s.at[phase, 1]
        first[...] = part.astype(BF16)
        copy = push(
            first, x_p.at[phase], x_send.at[phase, 0], x_recv.at[phase, 0], (seq, partner)
        )
        copy.wait_recv()
        pair = (first[...].astype(F32) + x_p[phase].astype(F32)).astype(BF16)
        second[...] = pair
        x_r[phase, chip] = pair
        arrive(
            [
                push(
                    second,
                    x_r.at[phase, chip],
                    x_send.at[phase, d],
                    x_recv.at[phase, d],
                    (seq, chip_peer(d)),
                )
                for d in ring_order(chips)
            ]
        )
        total = x_r[phase, 0].astype(F32)
        for index in range(1, chips):
            total = total + x_r[phase, index].astype(F32)
        return total

    barrier = pltpu.get_barrier_semaphore()
    for d in ring_order(nz):
        pl.semaphore_signal(barrier, inc=1, device_id=(y * nz + z_peer(d), e), device_id_type=MESH)
    for d in range(1, ny):
        pl.semaphore_signal(barrier, inc=1, device_id=(y_peer(d) * nz + z, e), device_id_type=MESH)
    pl.semaphore_signal(barrier, inc=1, device_id=(seq, partner), device_id_type=MESH)
    for d in range(1, chips):
        pl.semaphore_signal(barrier, inc=1, device_id=(seq, chip_peer(d)), device_id_type=MESH)

    def iota(shape, axis):
        return lax.broadcasted_iota(jnp.int32, shape, axis)

    def lane_of(count):
        return iota((count, LANES), 1)

    def by_head(columns):
        count = columns[0].shape[0]
        lane = lax.rem(lane_of(count), heads)
        spread = jnp.broadcast_to(columns[0], (count, LANES))
        for h in range(1, heads):
            spread = jnp.where(lane == h, columns[h], spread)
        return spread

    def thirds(values):
        high = values.astype(BF16).astype(F32)
        rest = values - high
        middle = rest.astype(BF16).astype(F32)
        return high, middle, rest - middle

    def pack_stats(top, total):
        group = lax.div(lane_of(top.shape[0]), heads)
        high, middle, low = thirds(top)
        total_high = total.astype(BF16).astype(F32)
        packed = jnp.where(group == 0, high, total - total_high)
        packed = jnp.where(group == 1, middle, packed)
        packed = jnp.where(group == 2, low, packed)
        packed = jnp.where(group == 3, total_high, packed)
        return packed

    def stat(values, group, h):
        lane = qcols + group * heads + h
        return values[..., lane : lane + 1]

    def unpack(values, h):
        top = (stat(values, 0, h) + stat(values, 1, h)) + stat(values, 2, h)
        total = stat(values, 3, h) + stat(values, 4, h)
        return top, total, values[..., h * HEAD_DIM : (h + 1) * HEAD_DIM]

    def column(row):
        size = row.shape[1]
        on = iota((size, size), 0) == iota((size, size), 1)
        return jnp.sum(jnp.where(on, row, 0.0), axis=1, keepdims=True)

    loads = [
        pltpu.make_async_copy(cache_hbm, cache_ref, load_sem.at[0]),
        pltpu.make_async_copy(ein_hbm, ein_ref, load_sem.at[1]),
        pltpu.make_async_copy(eout_hbm, eout_ref, load_sem.at[2]),
    ]
    for load in loads:
        load.start()

    tok = tok_ref[...].astype(F32)
    ones = jnp.ones((width, LANES), F32)
    normed = (tok * column(gains_ref[0:1, :])).astype(BF16)
    second_gain = column(gains_ref[1:2, :])
    q_part = dot(normed, qw_ref[...], FIRST)
    kv_weight = kvw_ref[...].astype(F32)
    k_part = dot(normed, kv_weight[:, 0, :].astype(BF16), FIRST)
    v_part = dot(normed, kv_weight[:, 1, :].astype(BF16), FIRST)
    squares = dot(tok * tok, ones, FIRST, HIGHEST)
    for part in range(ny):
        here = slice(part * ry, (part + 1) * ry)
        a_sy[part, :, 0:qcols] = q_part[here].astype(BF16)
        a_sy[part, :, qcols:kcols] = k_part[here].astype(BF16)
        a_sy[part, :, kcols:vcols] = v_part[here].astype(BF16)
        a_sy[part, :, vcols : vcols + LANES] = squares[here].astype(BF16)

    pl.semaphore_wait(barrier, (ny - 1) + (nz - 1) + chips)
    copies = y_exchange(a_sy, a_ry, 0)

    owners = []
    for p in range(blocks):
        place, start, owner = place_ref[p], 0, -1
        for r in range(requests):
            owner = owner + (place >= start).astype(jnp.int32)
            start = start + count_ref[r]
        owners.append(owner)
    same = [[(owners[p] == owners[q]).astype(jnp.int32) for q in range(blocks)] for p in range(blocks)]
    select, leads = [], []
    step = iota((8, rows), 0)
    wanted = iota((8, rows), 1)
    for p in range(blocks):
        chosen = (wanted == owners[p] + step * requests) & (step < steps)
        chosen = jnp.where(chosen, 1.0, 0.0)
        select.append(chosen)
        first = 1
        for q in range(p):
            first = first * (1 - same[p][q])
        leads.append(chosen * first.astype(F32) if p else chosen)
    select = jnp.concatenate(select, axis=0).astype(BF16)
    leads = jnp.concatenate(leads, axis=0).astype(BF16)

    part_sum = summed(a_sy[y], a_ry, copies)
    a_sz[...] = part_sum.reshape(nz, rp, part_sum.shape[1]).astype(BF16)
    copies = z_exchange(a_sz, a_rz, 0)
    arrive(copies)
    fresh = a_sz[z].astype(F32) + jnp.sum(a_rz[...].astype(F32), axis=0)
    attn_rms = lax.rsqrt(fresh[:, vcols : vcols + 1] / depth + EPSILON)
    own = (fresh[:, 0:vcols] * attn_rms).astype(BF16)
    a_g[y, z] = own
    gather(a_g, 1)
    fresh_rows = a_g[...].astype(F32).reshape(rows, vcols)[:, 0:qcols].astype(BF16)

    picked = dot(select, fresh_rows, MIDDLE)
    loads[0].wait()
    tops, totals, sums = [], [], []
    for p in range(blocks):
        here = slice(p * 8, (p + 1) * 8)
        block_query = jnp.concatenate(
            [picked[here, h * HEAD_DIM : (h + 1) * HEAD_DIM] for h in range(heads)], axis=0
        )
        scores = dot(block_query.astype(BF16), cache_ref[0, p], LAST) * scale
        top = jnp.max(scores, axis=1, keepdims=True)
        weights = jnp.exp(scores - top).astype(BF16)
        total = jnp.sum(weights.astype(F32), axis=1, keepdims=True)
        weighted = dot(weights, cache_ref[1, p], MIDDLE)
        alive = live_ref[p].astype(F32)
        top = by_head([top[h * 8 : (h + 1) * 8] for h in range(heads)])
        tops.append(top * alive + (1.0 - alive) * NEGATIVE)
        totals.append(by_head([total[h * 8 : (h + 1) * 8] for h in range(heads)]) * alive)
        sums.append(weighted * alive)
    joint, joint_sums = [], []
    for p in range(blocks):
        best = tops[p]
        for q in range(blocks):
            if q != p:
                apart = (1 - same[p][q]).astype(F32) * NEGATIVE
                best = jnp.maximum(best, tops[q] + apart)
        factor = jnp.exp(tops[p] - best)
        joint.append(best)
        joint_sums.append(
            jnp.concatenate(
                [sums[p][h * 8 : (h + 1) * 8] * factor[:, h : h + 1] for h in range(heads)]
                + [totals[p] * factor],
                axis=1,
            )
        )
    joint_sums = jnp.concatenate(joint_sums, axis=0)
    sums_high = joint_sums.astype(BF16)
    sums_low = (joint_sums - sums_high.astype(F32)).astype(BF16)
    local = dot(select, sums_high, FIRST) + dot(select, sums_low, FIRST)
    joint = jnp.concatenate(joint, axis=0)
    joint = jnp.where(lane_of(joint.shape[0]) < LANES // 2, joint, 1.0)
    local_top = sum(dot(leads, third.astype(BF16), FIRST) for third in reversed(thirds(joint)))
    present = local_top[:, LANES - 1 : LANES] > 0.5
    local_top = jnp.where(present, local_top, NEGATIVE)
    local_stats = pack_stats(local_top, local[:, qcols : qcols + LANES]).astype(BF16)
    for part in range(ny):
        here = slice(part * ry, (part + 1) * ry)
        e_sy[part, :, 0:qcols] = local[here, 0:qcols].astype(BF16)
        e_sy[part, :, qcols : qcols + LANES] = local_stats[here]
    copies = y_exchange(e_sy, e_ry, 2)

    own = own.astype(F32)
    new_rows = [a_g[s, z].astype(F32) for s in range(steps)]
    fresh_parts = []
    for h in range(heads):
        query = own[:, h * HEAD_DIM : (h + 1) * HEAD_DIM]
        scores = []
        for s in range(steps):
            score = jnp.sum(query * new_rows[s][:, qcols:kcols], axis=1, keepdims=True) * scale
            scores.append(jnp.where(y >= s, score, NEGATIVE))
        new_top = functools.reduce(jnp.maximum, scores)
        new_total, new_sum = 0.0, 0.0
        for s in range(steps):
            weight = jnp.where(y >= s, jnp.exp(scores[s] - new_top), 0.0)
            weight = weight.astype(BF16).astype(F32)
            new_total = new_total + weight
            new_sum = new_sum + weight * new_rows[s][:, kcols:vcols]
        fresh_parts.append((new_top, new_total, new_sum))

    arrive(copies)
    parts = [e_sy[y].astype(F32)] + [e_ry[slot].astype(F32) for slot in range(ny - 1)]
    tops, totals = [], []
    for h in range(heads):
        pieces = [unpack(values, h) for values in parts]
        top = functools.reduce(jnp.maximum, [piece[0] for piece in pieces])
        total, weighted = 0.0, 0.0
        for piece in pieces:
            factor = jnp.exp(piece[0] - top)
            total = total + factor * piece[1]
            weighted = weighted + factor * piece[2]
        tops.append(top)
        totals.append(total)
        e_sz[:, :, h * HEAD_DIM : (h + 1) * HEAD_DIM] = weighted.reshape(nz, rp, HEAD_DIM).astype(BF16)
    stats = pack_stats(by_head(tops), by_head(totals))
    e_sz[:, :, qcols : qcols + LANES] = stats.reshape(nz, rp, LANES).astype(BF16)
    copies = z_exchange(e_sz, e_rz, 2)
    arrive(copies)
    values = e_rz[...].astype(F32)
    mine = e_sz[z].astype(F32)
    attended = []
    for h in range(heads):
        tops, totals, sums = unpack(values, h)
        my_top, my_total, my_sum = unpack(mine, h)
        new_top, new_total, new_sum = fresh_parts[h]
        joined = jnp.maximum(jnp.maximum(jnp.max(tops, axis=0), my_top), new_top)
        factors = jnp.exp(tops - joined[None])
        my_factor = jnp.exp(my_top - joined)
        new_factor = jnp.exp(new_top - joined)
        total = jnp.sum(factors * totals, axis=0) + my_total * my_factor + new_total * new_factor
        weighted = jnp.sum(factors * sums, axis=0) + my_sum * my_factor + new_sum * new_factor
        attended.append(weighted / total)
    e_g[y, z] = jnp.concatenate(attended, axis=1).astype(BF16)
    gather(e_g, 3)
    attention = e_g[...].astype(F32).reshape(rows, qcols).astype(BF16)

    head_part = dot(ow_ref[...], attention, LAST)
    residual = tok + x_reduce(head_part, 0)

    hidden = (residual * second_gain).astype(BF16)
    hidden_float = hidden.astype(F32)
    loads[1].wait()
    chunks = [(k, c) for k in range(TOPK) for c in range(2)]
    masked = [None] * TOPK
    y_copies, z_copies = [], []

    def pass_on(j):
        part_sum = summed(b_sy[j, y], b_ry.at[j], y_copies[j])
        b_sz[j] = part_sum.reshape(nz, rp, ff).astype(BF16)
        z_copies.append(z_exchange(b_sz.at[j], b_rz.at[j], 5 + j))

    for j, (k, c) in enumerate(chunks):
        if c == 0:
            masked = jnp.concatenate(
                [
                    jnp.where(routes_ref[k : k + 1, :] == expert, hidden_float, 0.0)
                    for expert in range(experts)
                ],
                axis=0,
            ).astype(BF16)
        product = dot(masked, ein_ref[:, c].reshape(experts * width, ff), FIRST)
        for part in range(ny):
            b_sy[j, part] = product[part * ry : (part + 1) * ry].astype(BF16)
        y_copies.append(y_exchange(b_sy.at[j], b_ry.at[j], 5 + j))
        if j == 0:
            router = jnp.concatenate(
                [router_ref[...].astype(F32), jnp.zeros((LANES - experts, width), F32)], axis=0
            ).astype(BF16)
            logits = dot(hidden, router, (((0,), (1,)), ((), ())))
            squares = dot(residual * residual, ones, FIRST, HIGHEST)
            stats = jnp.where(lane_of(rows) < experts, logits, squares).astype(BF16)
            for part in range(ny):
                s_sy[part] = stats[part * ry : (part + 1) * ry]
            stat_copies = y_exchange(s_sy, s_ry, 4)
        if j == 1:
            part_sum = summed(s_sy[y], s_ry, stat_copies)
            s_sz[...] = part_sum.reshape(nz, rp, LANES).astype(BF16)
            stat_copies = z_exchange(s_sz, s_rz, 4)
        if j >= 2:
            pass_on(j - 2)
    pass_on(2)
    pass_on(3)
    arrive(stat_copies)
    stats = s_sz[z].astype(F32) + jnp.sum(s_rz[...].astype(F32), axis=0)
    moe_rms = lax.rsqrt(stats[:, LANES // 2 : LANES // 2 + 1] / depth + EPSILON)
    sigmoids = []
    for k in range(TOPK):
        wanted = jnp.full((rp, LANES), route_ref[k, seq * rp], jnp.int32)
        for row in range(1, rp):
            wanted = jnp.where(iota((rp, LANES), 0) == row, route_ref[k, seq * rp + row], wanted)
        logit = jnp.sum(jnp.where(lane_of(rp) == wanted, stats, 0.0), axis=1, keepdims=True) * moe_rms
        sigmoids.append(1.0 / (1.0 + jnp.exp(-logit)))
    z_held = []
    for k in range(TOPK):
        pair = []
        for c in range(2):
            j = 2 * k + c
            arrive(z_copies[j])
            pair.append((b_sz[j, z].astype(F32) + jnp.sum(b_rz[j].astype(F32), axis=0)) * moe_rms)
        active = pair[0] / (1.0 + jnp.exp(-pair[0])) * pair[1]
        b_g[k, y, z] = (active * (sigmoids[k] / (sigmoids[0] + sigmoids[1]))).astype(BF16)
        z_held.append(z_gather(b_g.at[k], 9 + k))
    y_held = []
    for k in range(TOPK):
        y_held.append(y_gather(b_g.at[k], 9 + k, z_held[k]))
    loads[2].wait()
    expert_part = jnp.zeros(residual.shape, F32)
    for k in range(TOPK):
        arrive(y_held[k])
        active = b_g[k].astype(F32).reshape(rows, ff).astype(BF16)
        product = dot(eout_ref[...].reshape(experts * width, ff), active, LAST)
        for expert in range(experts):
            expert_part = expert_part + jnp.where(
                routes_ref[k : k + 1, :] == expert,
                product[expert * width : (expert + 1) * width],
                0.0,
            )
    out_ref[...] = (residual + x_reduce(expert_part, 1)).astype(BF16)
    for copy in started:
        copy.wait_send()


def per_device(
    nx,
    seq_size,
    tokens,
    norm_gains,
    q_weight,
    kv_weight,
    out_weight,
    kv_cache,
    block_count,
    placement,
    block_live,
    router_weight,
    routes,
    expert_in,
    expert_out,
):
    width, rows = tokens.shape
    steps = rows // block_count.shape[0]
    ny, nz = steps, seq_size // steps
    rp = rows // seq_size
    ff = expert_in.shape[3]
    qcols = q_weight.shape[1]
    vcols = qcols + 2 * HEAD_DIM
    acols, ecols = vcols + LANES, qcols + LANES
    ry = rows // ny
    chunks = 2 * TOPK
    phases = 7 + chunks
    vmem = pl.BlockSpec(memory_space=pltpu.VMEM)
    smem = pl.BlockSpec(memory_space=pltpu.SMEM)
    held = pl.BlockSpec(memory_space=pl.ANY)
    return pl.pallas_call(
        functools.partial(kernel, (ny, nz, nx, width * seq_size, steps)),
        out_shape=jax.ShapeDtypeStruct((width, rows), BF16),
        in_specs=[smem] * 4 + [vmem] * 5 + [held, vmem, vmem, held, held],
        out_specs=vmem,
        scratch_shapes=[
            pltpu.VMEM((ny, ry, acols), BF16),
            pltpu.VMEM((ny - 1, ry, acols), BF16),
            pltpu.VMEM((nz, rp, acols), BF16),
            pltpu.VMEM((nz - 1, rp, acols), BF16),
            pltpu.VMEM((ny, nz, rp, vcols), BF16),
            pltpu.VMEM((ny, ry, ecols), BF16),
            pltpu.VMEM((ny - 1, ry, ecols), BF16),
            pltpu.VMEM((nz, rp, ecols), BF16),
            pltpu.VMEM((nz - 1, rp, ecols), BF16),
            pltpu.VMEM((ny, nz, rp, qcols), BF16),
            pltpu.VMEM((ny, ry, LANES), BF16),
            pltpu.VMEM((ny - 1, ry, LANES), BF16),
            pltpu.VMEM((nz, rp, LANES), BF16),
            pltpu.VMEM((nz - 1, rp, LANES), BF16),
            pltpu.VMEM((chunks, ny, ry, ff), BF16),
            pltpu.VMEM((chunks, ny - 1, ry, ff), BF16),
            pltpu.VMEM((chunks, nz, rp, ff), BF16),
            pltpu.VMEM((chunks, nz - 1, rp, ff), BF16),
            pltpu.VMEM((TOPK, ny, nz, rp, ff), BF16),
            pltpu.VMEM((2, 2, width, rows), BF16),
            pltpu.VMEM((2, width, rows), BF16),
            pltpu.VMEM((2, nx // 2, width, rows), BF16),
            pltpu.SemaphoreType.DMA((phases, ny - 1)),
            pltpu.SemaphoreType.DMA((phases, nz - 1)),
            pltpu.SemaphoreType.DMA((2, nx // 2)),
            pltpu.SemaphoreType.DMA((phases, ny - 1)),
            pltpu.SemaphoreType.DMA((phases, nz - 1)),
            pltpu.SemaphoreType.DMA((2, nx // 2)),
            pltpu.VMEM(kv_cache.shape, BF16),
            pltpu.VMEM(expert_in.shape, BF16),
            pltpu.VMEM(expert_out.shape, BF16),
            pltpu.SemaphoreType.DMA((3,)),
        ],
        compiler_params=pltpu.CompilerParams(
            collective_id=0, has_side_effects=True, vmem_limit_bytes=60 * 1024 * 1024
        ),
    )(
        block_count,
        placement,
        block_live,
        routes.T,
        tokens,
        norm_gains,
        q_weight,
        kv_weight,
        out_weight,
        kv_cache,
        router_weight.T,
        routes.T,
        expert_in,
        expert_out,
    )


def solution(mesh):
    return jax.shard_map(
        functools.partial(per_device, mesh.shape["exp"], mesh.shape["seq"]),
        mesh=mesh,
        in_specs=(
            P("seq", None),
            P(None, "seq"),
            P("seq", "exp"),
            P("seq", None, "exp"),
            P("seq", "exp"),
            P(None, "seq", None, "exp"),
            P(),
            P("seq"),
            P("seq"),
            P("seq", None),
            P(),
            P(None, None, "seq", "exp"),
            P(None, "seq", "exp"),
        ),
        out_specs=P("seq", None),
        check_vma=False,
    )
```
